128 devices in a mesh: box: 64 (over y, z_hi, x, core), dir: 2 (over z_lo).
Axes of the slice: x: 4, y: 4, z: 4 (z_hi: 2, z_lo: 2; z = z_hi * 2 + z_lo), core: 2. Of those that a mesh axis runs over, the one named last changes fastest.
Arguments:
- sources: bfloat16 [256, 2, 32, 256], P('box'), may hold values from -6 to 6
- encode: bfloat16 [2, 1024, 256], P(None, 'dir'), may hold values from -0.375 to 0.375
- kernel: float32 [1024, 2, 16, 128], P(('dir', 'box')), may hold values from -0.25 to 0.25
- decode: bfloat16 [2, 1024, 256], P(None, 'dir'), may hold values from -0.1875 to 0.1875
- near_blocks: bfloat16 [256, 28, 2, 256, 256], P('box', 'dir'), may hold values from -0.078125 to 0.078125
- near_list: int32 [256, 28], P('box', 'dir'), may hold values from 0 to 255, as said below
- near_mask: int32 [256, 28], P('box', 'dir'), may hold values from 0 to 1, as said below
- box_cell: int32 [256], replicated, may hold values from 0 to 255, as said below
Outputs:
- product: float32 [256, 2, 32, 256], P('box', None, None, 'dir')
The draws below stay inside these ranges and needn't reach their ends.
Inputs may be any that keep to these rules, and one draw needn't show every extreme that they name: A permutation of the cells: box b lies in cell box_cell[b] = (ix * 8 + iy) * 4 + iz of the 8 x 8 x 4 grid. Where near_mask[b, s] is 1, near_list[b, s] is the box whose cell differs from box b's cell by -1, 0 or 1 along each dimension, each such box named in one slot of b (b itself included); elsewhere any box. `near_mask`: 1 exactly where the slot names a cell inside the grid; at least one slot of every box is 0.
All inputs are finite; a program needn't handle non-finite values.
Results may differ from the reference program's by a relative error of at most 0.0027.
Values may be sent and summed in bfloat16 or wider, within the bound.
A program may use at most 128 MiB of HBM per device.

```python
import jax
import jax.numpy as jnp
from jax import lax

P_SIZE = 256
K = 1024
R = 32
SLOTS = 28
GY = 8
GZ = 4
BOXES = 256
GX = 8


def grid_layout(key):
    cells = jax.random.permutation(jax.random.fold_in(key, 101), BOXES).astype(jnp.int32)
    at_cell = jnp.zeros((BOXES,), jnp.int32).at[cells].set(jnp.arange(BOXES, dtype=jnp.int32))
    code = jnp.arange(27, dtype=jnp.int32)
    table = jnp.stack([code // 9 - 1, code // 3 % 3 - 1, code % 3 - 1], axis=1)
    filler = jnp.full((SLOTS - 27, 3), 2 * BOXES, jnp.int32)
    table = jnp.concatenate([table, filler], axis=0)
    box_keys = jax.random.split(jax.random.fold_in(key, 102), BOXES)
    orders = jax.vmap(lambda single: jax.random.permutation(single, SLOTS))(box_keys)
    stepped = table[orders]
    cell_x = cells // (GY * GZ)
    cell_y = cells // GZ % GY
    cell_z = cells % GZ
    next_x = cell_x[:, None] + stepped[:, :, 0]
    next_y = cell_y[:, None] + stepped[:, :, 1]
    next_z = cell_z[:, None] + stepped[:, :, 2]
    inside = (next_x >= 0) & (next_x < GX) & (next_y >= 0) & (next_y < GY) & (next_z >= 0) & (next_z < GZ)
    next_cell = (jnp.clip(next_x, 0, GX - 1) * GY + jnp.clip(next_y, 0, GY - 1)) * GZ + jnp.clip(next_z, 0, GZ - 1)
    filler_boxes = jax.random.randint(jax.random.fold_in(key, 103), (BOXES, SLOTS), 0, BOXES).astype(jnp.int32)
    neighbours = jnp.where(inside, at_cell[next_cell], filler_boxes).astype(jnp.int32)
    return (cells, neighbours, inside.astype(jnp.int32))


def draw_near_list(key, part):
    return grid_layout(key)[1]


def draw_near_mask(key, part):
    return grid_layout(key)[2]


def draw_box_cell(key, part):
    return grid_layout(key)[0]


def block_levels(key, shape, cuts, smallest, top_value):
    def one(dim, blocks):
        steps = jax.random.uniform(jax.random.fold_in(jax.random.fold_in(key, 6), dim), (blocks,), jnp.float32, smallest / len(cuts), top_value / len(cuts))
        return jnp.repeat(jnp.exp(steps), shape[dim] // blocks).reshape((-1,) + (1,) * (len(shape) - dim - 1))

    loudness = one(*cuts[0])
    for cut in cuts[1:]:
        loudness = loudness * one(*cut)
    return loudness


def bell_draw(own_key, dims, width, limit, cuts=(), kind=jnp.bfloat16):
    result = width * jax.random.normal(own_key, dims, jnp.float32)
    if cuts:
        result = result * block_levels(own_key, dims, cuts, -0.22, 0.18)
    return jnp.clip(result, -limit, limit).astype(kind)


def setup_inputs(seed: int = 0) -> dict:
    arg_keys = jax.random.split(jax.random.key(seed), 9)
    sources = bell_draw(arg_keys[0], (BOXES, 2, R, P_SIZE), 1.0, 6.0, ((0, 64),))
    encode = bell_draw(arg_keys[1], (2, K, P_SIZE), P_SIZE ** -0.5, 0.375, ((1, 2),))
    kernel = bell_draw(arg_keys[2], (K, 2, 2 * GX, 4 * GY * GZ), (2 * BOXES) ** -0.5, 0.25, ((0, 128),), jnp.float32)
    decode = bell_draw(arg_keys[3], (2, K, P_SIZE), K ** -0.5, 0.1875, ((1, 2),))
    near_blocks = bell_draw(arg_keys[4], (BOXES, SLOTS, 2, P_SIZE, P_SIZE), (27 * P_SIZE) ** -0.5, 0.078125, ((0, 64), (1, 2)))
    near_list = draw_near_list(jax.random.fold_in(arg_keys[8], 71), 0)
    near_mask = draw_near_mask(jax.random.fold_in(arg_keys[8], 71), 0)
    box_cell = draw_box_cell(jax.random.fold_in(arg_keys[8], 71), 0)
    return dict(sources=sources, encode=encode, kernel=kernel, decode=decode, near_blocks=near_blocks, near_list=near_list, near_mask=near_mask, box_cell=box_cell)


def near_line(length):
    halfway = length // 2
    index = jnp.arange(length, dtype=jnp.int32)
    offset = jnp.where(index < halfway, index, index - length)
    return jnp.abs(offset) <= 1


def keep_mask(double_x, double_y, double_z):
    near_x = near_line(double_x)
    near_plane = (near_line(double_y)[:, None] & near_line(double_z)[None, :]).reshape(-1)
    return jnp.where(near_x[:, None] & near_plane[None, :], 0.0, 1.0).astype(jnp.float32)


def contract_last(left, right):
    return lax.dot_general(left, right, (((1,), (1,)), ((), ())), preferred_element_type=jnp.float32)


def contract_first(left, right):
    return lax.dot_general(left, right, (((0,), (0,)), ((), ())), preferred_element_type=jnp.float32)


def reference(sources, encode, kernel, decode, near_blocks, near_list, near_mask, box_cell):
    flat_re = sources[:, 0].reshape(BOXES * R, P_SIZE)
    flat_im = sources[:, 1].reshape(BOXES * R, P_SIZE)
    coded_re = contract_last(encode[0], flat_re) - contract_last(encode[1], flat_im)
    coded_im = contract_last(encode[0], flat_im) + contract_last(encode[1], flat_re)
    coded = lax.complex(coded_re, coded_im).reshape(K, BOXES, R).transpose(0, 2, 1)
    placed = jnp.zeros((K, R, BOXES), coded.dtype).at[:, :, box_cell].set(coded)
    placed = placed.reshape(K, R, GX, GY, GZ)
    padded = jnp.pad(placed, ((0, 0), (0, 0), (0, GX), (0, GY), (0, GZ)))
    keep = keep_mask(2 * GX, 2 * GY, 2 * GZ)
    kern = lax.complex(kernel[:, 0] * keep, kernel[:, 1] * keep).reshape(K, 2 * GX, 2 * GY, 2 * GZ)
    spectrum = jnp.fft.fftn(padded, axes=(2, 3, 4)) * jnp.fft.fftn(kern, axes=(1, 2, 3))[:, None]
    far = jnp.fft.ifftn(spectrum, axes=(2, 3, 4))[:, :, :GX, :GY, :GZ].reshape(K, R, BOXES)
    far_box = far[:, :, box_cell]
    farb_re = jnp.real(far_box).astype(jnp.bfloat16).reshape(K, R * BOXES)
    farb_im = jnp.imag(far_box).astype(jnp.bfloat16).reshape(K, R * BOXES)
    far_re = contract_first(farb_re, decode[0]) - contract_first(farb_im, decode[1])
    far_im = contract_first(farb_im, decode[0]) + contract_first(farb_re, decode[1])
    far_part = jnp.stack([far_re.reshape(R, BOXES, P_SIZE), far_im.reshape(R, BOXES, P_SIZE)], axis=0).transpose(2, 0, 1, 3)

    def near_box(packed):
        blocks, source_ids, marks = packed
        picked = sources[source_ids].astype(jnp.float32) * marks.astype(jnp.float32)[:, None, None, None]
        blocks = blocks.astype(jnp.float32)
        near_re = jnp.einsum("spq,srq->rp", blocks[:, 0], picked[:, 0]) - jnp.einsum("spq,srq->rp", blocks[:, 1], picked[:, 1])
        near_im = jnp.einsum("spq,srq->rp", blocks[:, 0], picked[:, 1]) + jnp.einsum("spq,srq->rp", blocks[:, 1], picked[:, 0])
        return jnp.stack([near_re, near_im], axis=0)

    near_part = lax.map(near_box, (near_blocks, near_list, near_mask))
    return far_part + near_part
```

```python
import functools

import jax
import jax.numpy as jnp
import numpy as np
from jax import lax
from jax.experimental import pallas as pl
from jax.experimental.pallas import tpu as pltpu
from jax.sharding import PartitionSpec as P

MESH = pl.DeviceIdType.MESH
BF = jnp.bfloat16
F32 = jnp.float32

NB = 64
PER = 4
KD = 8
RHS = 32
SLOTS = 14
SZ = 256

ZX = 0
P1 = 1
F1 = 5
P2 = 7
F2 = 23
SIB = 31
HALF = 47
OFFS = (0, -1, 1, 2)


def input_order():
    order = np.zeros(256, np.int32)
    for w in range(2):
        for j in range(128):
            h, c, p2, p1, z = j // 64, j // 32 % 2, j // 8 % 4, j // 2 % 4, j % 2
            y, x = (p2, p1) if h == 0 else (p1, p2)
            order[w * 128 + j] = (((y * 2 + z) * 4 + x) * 2 + c) * 4 + 2 * h + w
    return order


def output_order():
    return np.array([4 * d + q for q in range(4) for d in range(64)], np.int32)


def dot_nt(a, b):
    return lax.dot_general(a, b, (((1,), (1,)), ((), ())), preferred_element_type=F32)


def body(idx_ref, src_ref, enc_ref, ker_ref, dec_ref, cols_ref, nb_hbm, out_ref,
         S, W, TT, D, V, SEND, R, NBV, NEAR, PS, PR, QI, QO,
         ssem, rsem, lsem, nsem, a2s, a2r, pss, psr):
    bi = lax.axis_index("box")
    zl = lax.axis_index("dir")
    c = lax.rem(bi, 2)
    x = lax.rem(bi // 2, 4)
    zh = lax.rem(bi // 8, 2)
    y = bi // 16

    def dev(y_, zh_, x_, c_):
        return ((y_ * 2 + zh_) * 4 + x_) * 2 + c_

    def wrap(v):
        return lax.rem(v + 8, 4)

    zpart = (dev(y, 1 - zh, x, c), 1 - zl)
    sib = (dev(y, zh, x, 1 - c), zl)
    partner = (bi, 1 - zl)

    nb_copies = [pltpu.make_async_copy(nb_hbm.at[q], NBV.at[q], nsem.at[q]) for q in range(PER)]
    for cp in nb_copies:
        cp.start()

    bar = pltpu.get_barrier_semaphore()

    def greet(t, _):
        pl.semaphore_signal(bar, inc=1, device_id=(lax.rem(bi + t, NB), zl), device_id_type=MESH)
        return 0

    lax.fori_loop(1, NB, greet, 0)
    pl.semaphore_signal(bar, inc=1, device_id=zpart, device_id_type=MESH)
    pl.semaphore_signal(bar, inc=1, device_id=partner, device_id_type=MESH)
    pl.semaphore_wait(bar, NB + 1)

    def pos(h):
        return (x, y) if h == 0 else (y, x)

    def ring(h, level, side):
        step = 1 if side == 0 else -1
        along_x = (h == 0) == (level == 1)
        if along_x:
            return (dev(y, zh, wrap(x + step), c), zl)
        return (dev(wrap(y + step), zh, x, c), zl)

    def sub(h, c_, p2, p1, z):
        return h * 64 + c_ * 32 + p2 * 8 + p1 * 2 + z

    def zof(which):
        return zh if which == 0 else 1 - zh

    def at(j, n=1):
        return S.at[pl.ds(2 * j, 2 * n)]

    started = []

    def send(h, num, j, device, n=1, src=None):
        cp = pltpu.make_async_remote_copy(
            src_ref=at(j, n) if src is None else src, dst_ref=at(j, n),
            send_sem=ssem.at[h * HALF + num], recv_sem=rsem.at[h * HALF + num],
            device_id=device, device_id_type=MESH)
        cp.start()
        started.append(cp)

    def recv(h, num, n=1):
        k = h * HALF + num
        pltpu.make_async_copy(S.at[pl.ds(0, 2 * n)], S.at[pl.ds(0, 2 * n)], rsem.at[k]).wait()

    def p2_send(h, piece, which, src=None):
        a, b = pos(h)
        j = sub(h, c, b, wrap(a + OFFS[piece]), zof(which))
        for side in (0, 1):
            send(h, P2 + 4 * piece + 2 * which + side, j, ring(h, 2, side), src=src)

    def encode(j0):
        rows = S[pl.ds(2 * j0, 4)].reshape(256, SZ)
        o = dot_nt(enc_ref[...], rows)
        top, low = o[0:8], o[8:16]
        lane = lax.broadcasted_iota(jnp.int32, (8, 128), 1) % 64
        for half in range(2):
            t = top[:, 128 * half:128 * half + 128]
            u = low[:, 128 * half:128 * half + 128]
            turned = jnp.where(lane < 32, -pltpu.roll(u, 96, 1), pltpu.roll(u, 32, 1))
            W[pl.ds(pl.multiple_of(8 * j0 + 8 * half, 8), 8), :] = t + turned

    def sib_send(h, drow, piece):
        a, b = pos(h)
        j0 = sub(h, c, wrap(b + OFFS[drow]), wrap(a + OFFS[piece]), 0)
        send(h, SIB + 4 * drow + piece, j0, sib, n=2)
        encode(j0)

    def p1_recv(h, which, side):
        recv(h, P1 + 2 * which + side)

    local = []
    for h in (0, 1):
        a, b = pos(h)
        own = sub(h, c, b, a, zh)
        src = src_ref.at[pl.ds(2 * h, 2)]
        send(h, ZX, own, zpart, src=src)
        for side in (0, 1):
            send(h, P1 + side, own, ring(h, 1, side), src=src)
        p2_send(h, 0, 0, src=src)
        cp = pltpu.make_async_copy(src, at(own), lsem.at[h])
        cp.start()
        local.append(cp)

    S[pl.ds(256, 2)] = jnp.zeros((2, 64, SZ), BF)
    cin = cols_ref[:, 0:1]
    cout = cols_ref[:, 1:2]
    QI[...] = jnp.where(lax.broadcasted_iota(jnp.int32, (256, 256), 1) == cin, 1.0, 0.0).astype(BF)
    QO[...] = jnp.where(lax.broadcasted_iota(jnp.int32, (256, 512), 1) == cout, 1.0, 0.0).astype(BF)

    def build_d(mine):
        col = pl.multiple_of(128 * (zl if mine else 1 - zl), 128)
        dr = dec_ref[0, :, pl.ds(col, 128)].astype(F32).reshape(64, 1, 8, 128)
        di = dec_ref[1, :, pl.ds(col, 128)].astype(F32).reshape(64, 1, 8, 128)
        left = jnp.concatenate([dr, -di], axis=1).reshape(1024, 128)
        right = jnp.concatenate([di, dr], axis=1).reshape(1024, 128)
        D[0 if mine else 1] = jnp.concatenate([left, right], axis=1).astype(BF)

    def build_t(k):
        d_i = lax.broadcasted_iota(jnp.int32, (16, 128), 0)
        l_i = lax.broadcasted_iota(jnp.int32, (16, 128), 1)
        ly, lz = l_i // 8, l_i % 8
        near = (((d_i <= 1) | (d_i == 15)) & ((ly <= 1) | (ly == 15)) & ((lz <= 1) | (lz == 7)))
        lane = lax.broadcasted_iota(jnp.int32, (8, 128), 1)
        for ri in range(2):
            row = jnp.where(near, 0.0, ker_ref[k, ri])
            row = jnp.where(lz < 4, row, pltpu.roll(row, 120, 1))
            pieces = {}
            for dx in range(-7, 8):
                base = jnp.broadcast_to(row[dx % 16:dx % 16 + 1, :], (8, 128))
                pieces[dx] = [pltpu.roll(base, sz, 1, stride=8, stride_axis=0) for sz in range(4)]
            pairs = {}
            for d in range(-7, 7):
                pairs[d] = [jnp.where(lane < 64, pieces[d][s], pltpu.roll(pieces[d + 1][s], 64, 1))
                            for s in range(4)]
            wide = jnp.concatenate([
                jnp.concatenate([pairs[2 * j - sx][s] for j in range(4)], axis=1)
                for sx in range(8) for s in range(4)], axis=0)
            hi = wide.astype(BF)
            lo = (wide - hi.astype(F32)).astype(BF)
            for part, val in enumerate((hi, lo)):
                first = dot_nt(QO[...], val).astype(BF)
                TT[k, part, ri] = dot_nt(first, QI[...]).astype(BF)

    build_d(False)
    build_d(True)
    for cp in local:
        cp.wait()

    for h in (0, 1):
        a, b = pos(h)
        recv(h, ZX)
        other = sub(h, c, b, a, 1 - zh)
        for side in (0, 1):
            send(h, P1 + 2 + side, other, ring(h, 1, side))
        p2_send(h, 0, 1)
        sib_send(h, 0, 0)

    for h in (0, 1):
        a, b = pos(h)
        for side in (0, 1):
            p1_recv(h, 0, side)
        send(h, F1, sub(h, c, b, wrap(a - 1), zh), ring(h, 1, 0))
        p2_send(h, 1, 0)
        p2_send(h, 2, 0)

    def step_t(k, _):
        build_t(k)
        return 0

    lax.fori_loop(0, 2, step_t, 0)

    for h in (0, 1):
        a, b = pos(h)
        for side in (0, 1):
            recv(h, P2 + side)
        send(h, F2, sub(h, c, wrap(b - 1), a, zh), ring(h, 2, 0))

    for h in (0, 1):
        a, b = pos(h)
        for side in (0, 1):
            p1_recv(h, 1, side)
        send(h, F1 + 1, sub(h, c, b, wrap(a + 1), 1 - zh), ring(h, 1, 1))
        p2_send(h, 1, 1)
        p2_send(h, 2, 1)
        sib_send(h, 0, 1)
        sib_send(h, 0, 2)

    lax.fori_loop(2, 4, step_t, 0)

    for h in (0, 1):
        a, b = pos(h)
        for side in (0, 1):
            recv(h, P2 + 2 + side)
        send(h, F2 + 1, sub(h, c, wrap(b + 1), a, 1 - zh), ring(h, 2, 1))
        sib_send(h, 1, 0)
        sib_send(h, 2, 0)

    for h in (0, 1):
        for side in (0, 1):
            recv(h, F1 + side)
        p2_send(h, 3, 0)
        p2_send(h, 3, 1)
        sib_send(h, 0, 3)

    lax.fori_loop(4, 6, step_t, 0)

    def relay(h, piece):
        a, b = pos(h)
        p1 = wrap(a + OFFS[piece])
        for which in (0, 1):
            for side in (0, 1):
                recv(h, P2 + 4 * piece + 2 * which + side)
            if which == 0:
                send(h, F2 + 2 * piece, sub(h, c, wrap(b - 1), p1, zh), ring(h, 2, 0))
            else:
                send(h, F2 + 2 * piece + 1, sub(h, c, wrap(b + 1), p1, 1 - zh), ring(h, 2, 1))
        sib_send(h, 1, piece)
        sib_send(h, 2, piece)

    for piece in (1, 2):
        for h in (0, 1):
            relay(h, piece)
    lax.fori_loop(6, 8, step_t, 0)
    for h in (0, 1):
        relay(h, 3)

    for piece in range(4):
        for h in (0, 1):
            for side in (0, 1):
                recv(h, F2 + 2 * piece + side)
            sib_send(h, 3, piece)

    for drow in range(4):
        for piece in range(4):
            for h in (0, 1):
                a, b = pos(h)
                recv(h, SIB + 4 * drow + piece, n=2)
                encode(sub(h, 1 - c, wrap(b + OFFS[drow]), wrap(a + OFFS[piece]), 0))

    for cp in started:
        cp.wait_send()

    lane64 = lax.broadcasted_iota(jnp.int32, (256, 64), 1)
    quarter = lax.broadcasted_iota(jnp.int32, (64, 128), 1) // 32

    def translate(k, _):
        v = W[pl.ds(k, 128, stride=8), :]
        e = jnp.concatenate([v[:, 0:64], v[:, 64:128]], axis=0)
        hi = e.astype(BF)
        lo = (e - hi.astype(F32)).astype(BF)
        t_hi = TT[k, 0].reshape(512, 256)
        t_lo = TT[k, 1].reshape(512, 256)
        nn = (((1,), (0,)), ((), ()))
        f = lax.dot_general(t_hi, hi, nn, preferred_element_type=F32)
        f = f + lax.dot_general(t_hi, lo, nn, preferred_element_type=F32)
        f = f + lax.dot_general(t_lo, hi, nn, preferred_element_type=F32)
        fr, fi = f[0:256], f[256:512]
        swapped = jnp.concatenate([fi[:, 32:64], fi[:, 0:32]], axis=1)
        far = fr + jnp.where(lane64 < 32, -swapped, swapped)
        far = jnp.concatenate([far, far], axis=1)
        far_sw = pltpu.roll(far, 32, 1)
        for ri in range(2):
            val = None
            for q in range(4):
                use = far if (q - ri) % 2 == 0 else far_sw
                block = use[64 * q:64 * q + 64]
                val = block if val is None else jnp.where(quarter == q, block, val)
            V[pl.ds(8 * ri + k, 64, stride=16), :] = val
        return 0

    lax.fori_loop(0, KD, translate, 0)
    SEND[...] = V[...].astype(BF).reshape(64, 16, 128)
    R[pl.ds(bi, 1)] = SEND[pl.ds(bi, 1)]

    def scatter(t, _):
        dst = lax.rem(bi + t, NB)
        pltpu.make_async_remote_copy(
            src_ref=SEND.at[dst], dst_ref=R.at[bi], send_sem=a2s.at[0], recv_sem=a2r.at[0],
            device_id=(dst, zl), device_id_type=MESH).start()
        return 0

    lax.fori_loop(1, NB, scatter, 0)

    def near_box(q, _):
        blocks = NBV[q]
        xs = jnp.concatenate([S[idx_ref[q, s]] for s in range(SLOTS)], axis=1)
        bs = jnp.concatenate([blocks[s] for s in range(SLOTS)], axis=1)
        n = dot_nt(xs, bs)
        NEAR[q, 0] = n[0:32, 0:256] - n[32:64, 256:512]
        NEAR[q, 1] = n[32:64, 0:256] + n[0:32, 256:512]
        return 0

    for cp in nb_copies:
        cp.wait()
    lax.fori_loop(0, PER, near_box, 0)

    whole = R.at[pl.ds(0, NB - 1)]
    pltpu.make_async_copy(whole, whole, a2r.at[0]).wait()
    got = R[...].reshape(1024, 128)

    def decode(which):
        return lax.dot_general(got, D[which], (((0,), (0,)), ((), ())), preferred_element_type=F32)

    def combine(which, target):
        far = decode(which)
        col = pl.multiple_of(128 * (zl if which == 0 else 1 - zl), 128)
        for q in range(4):
            for ro in range(2):
                target[q, ro] = (far[32 * q:32 * q + 32, 128 * ro:128 * ro + 128]
                                 + NEAR[q, ro, :, pl.ds(col, 128)])

    combine(1, PS)
    last = pltpu.make_async_remote_copy(
        src_ref=PS, dst_ref=PR, send_sem=pss.at[0], recv_sem=psr.at[0],
        device_id=partner, device_id_type=MESH)
    last.start()
    combine(0, out_ref)
    sent = SEND.at[pl.ds(0, NB - 1)]
    pltpu.make_async_copy(sent, sent, a2s.at[0]).wait()
    last.wait()
    out_ref[...] += PR[...]


def on_device(sources, encode, kernel, decode, near_blocks, near_list, near_mask, box_cell):
    bi = lax.axis_index("box")
    enc = lax.dynamic_slice_in_dim(encode, bi * KD, KD, axis=1).reshape(2 * KD, SZ)
    v = near_list
    w, h, c = v % 2, v // 2 % 2, v // 4 % 2
    x, z, y = v // 8 % 4, v // 32 % 2, v // 64
    p2 = jnp.where(h == 1, x, y)
    p1 = jnp.where(h == 1, y, x)
    idx = 2 * (h * 64 + c * 32 + p2 * 8 + p1 * 2 + z) + w
    idx = jnp.where(near_mask == 1, idx, 256)
    cx, cy, cz = box_cell // 32, box_cell // 4 % 8, box_cell % 4
    cell_in = cx * 32 + cz * 8 + cy
    cell_out = cx * 64 + cy * 8 + cz
    cols = jnp.stack([cell_in[input_order()], cell_out[output_order()]], axis=1)
    vm = pl.BlockSpec(memory_space=pltpu.VMEM)
    n_sem = 2 * HALF
    return pl.pallas_call(
        body,
        out_shape=jax.ShapeDtypeStruct((PER, 2, RHS, 128), F32),
        in_specs=[pl.BlockSpec(memory_space=pltpu.SMEM), vm, vm, vm, vm, vm,
                  pl.BlockSpec(memory_space=pl.ANY)],
        out_specs=vm,
        scratch_shapes=[
            pltpu.VMEM((258, 64, SZ), BF),
            pltpu.VMEM((1024, 128), F32),
            pltpu.VMEM((KD, 2, 2, 256, 256), BF),
            pltpu.VMEM((2, 1024, 256), BF),
            pltpu.VMEM((1024, 128), F32),
            pltpu.VMEM((NB, 16, 128), BF),
            pltpu.VMEM((NB, 16, 128), BF),
            pltpu.VMEM((PER, SLOTS, 512, SZ), BF),
            pltpu.VMEM((PER, 2, RHS, SZ), F32),
            pltpu.VMEM((PER, 2, RHS, 128), F32),
            pltpu.VMEM((PER, 2, RHS, 128), F32),
            pltpu.VMEM((256, 256), BF),
            pltpu.VMEM((256, 512), BF),
            pltpu.SemaphoreType.DMA((n_sem,)),
            pltpu.SemaphoreType.DMA((n_sem,)),
            pltpu.SemaphoreType.DMA((2,)),
            pltpu.SemaphoreType.DMA((PER,)),
            pltpu.SemaphoreType.DMA((1,)),
            pltpu.SemaphoreType.DMA((1,)),
            pltpu.SemaphoreType.DMA((1,)),
            pltpu.SemaphoreType.DMA((1,)),
        ],
        compiler_params=pltpu.CompilerParams(
            collective_id=0, has_side_effects=True, vmem_limit_bytes=56 * 2**20),
        name="fmm",
    )(idx, sources.reshape(PER, 64, SZ), enc, kernel, decode, cols,
      near_blocks.reshape(PER, SLOTS, 512, SZ))


def solution(mesh):
    in_specs = (
        P("box", None, None, None),
        P(None, "dir", None),
        P(("dir", "box"), None, None, None),
        P(None, "dir", None),
        P("box", "dir", None, None, None),
        P("box", "dir"),
        P("box", "dir"),
        P(),
    )
    return jax.shard_map(
        on_device, mesh=mesh, in_specs=in_specs, out_specs=P("box", None, None, "dir"),
        check_vma=False)
```

```python
import jax
import jax.numpy as jnp
from jax import lax
from jax.experimental import pallas as pl
from jax.experimental.pallas import tpu as pltpu
from jax.sharding import PartitionSpec as P

MESH = pl.DeviceIdType.MESH
BF = jnp.bfloat16
F32 = jnp.float32

NB = 64
PER = 4
KD = 8
RHS = 32
SLOTS = 14
SZ = 256

ZX = 0
P1 = 1
F1 = 5
P2 = 7
F2 = 23
SIB = 31
HALF = 47
OFFS = (0, -1, 1, 2)


def box_of_input(i):
    w, j = i // 128, i % 128
    h, c, p2, p1, z = j // 64, j // 32 % 2, j // 8 % 4, j // 2 % 4, j % 2
    y = jnp.where(h == 0, p2, p1)
    x = jnp.where(h == 0, p1, p2)
    return (((y * 2 + z) * 4 + x) * 2 + c) * 4 + 2 * h + w


def slot_of_box(v):
    w, h, c = lax.rem(v, 2), lax.rem(v // 2, 2), lax.rem(v // 4, 2)
    x, z, y = lax.rem(v // 8, 4), lax.rem(v // 32, 2), v // 64
    first = 8 * y + 2 * x
    second = 8 * x + 2 * y
    return 2 * (h * 64 + c * 32 + jnp.where(h == 1, second, first) + z) + w


def dot_nt(a, b):
    return lax.dot_general(a, b, (((1,), (1,)), ((), ())), preferred_element_type=F32)


def body(list_ref, mask_ref, cell_ref, src_ref, enc_hbm, ker_hbm, dec_hbm, nb_hbm, out_ref,
         S, W, TT, D, V, SEND, R, NBV, NEAR, NS, NR, FS, FR, QI, QO, BASE, ENC2, E16, KER, DEC,
         ssem, rsem, lsem, nsem, isem, a2s, a2r, pss, psr, ready):
    bi = lax.axis_index("box")
    zl = lax.axis_index("dir")
    c = lax.rem(bi, 2)
    x = lax.rem(bi // 2, 4)
    zh = lax.rem(bi // 8, 2)
    y = bi // 16

    def dev(y_, zh_, x_, c_):
        return ((y_ * 2 + zh_) * 4 + x_) * 2 + c_

    def wrap(v):
        return lax.rem(v + 8, 4)

    zpart = (dev(y, 1 - zh, x, c), 1 - zl)
    sib = (dev(y, zh, x, 1 - c), zl)
    partner = (bi, 1 - zl)

    right, left = (dev(y, zh, wrap(x + 1), c), zl), (dev(y, zh, wrap(x - 1), c), zl)
    up, down = (dev(wrap(y + 1), zh, x, c), zl), (dev(wrap(y - 1), zh, x, c), zl)
    bar = pltpu.get_barrier_semaphore()
    for other in (right, left, up, down, zpart, sib, partner):
        pl.semaphore_signal(bar, inc=1, device_id=other, device_id_type=MESH)

    in_copies = [
        pltpu.make_async_copy(enc_hbm.at[:, pl.ds(pl.multiple_of(16 * (bi // 2), 16), 16), :], ENC2, isem.at[0]),
        pltpu.make_async_copy(ker_hbm, KER, isem.at[1]),
        pltpu.make_async_copy(dec_hbm, DEC, isem.at[2])]
    for cp in in_copies:
        cp.start()
    nb_copies = [pltpu.make_async_copy(nb_hbm.at[q], NBV.at[q], nsem.at[q]) for q in range(PER)]
    for cp in nb_copies:
        cp.start()
    pl.semaphore_wait(bar, 7)

    def pos(h):
        return (x, y) if h == 0 else (y, x)

    def ring(h, level, side):
        step = 1 if side == 0 else -1
        along_x = (h == 0) == (level == 1)
        if along_x:
            return (dev(y, zh, wrap(x + step), c), zl)
        return (dev(wrap(y + step), zh, x, c), zl)

    def sub(h, c_, p2, p1, z):
        return h * 64 + c_ * 32 + p2 * 8 + p1 * 2 + z

    def zof(which):
        return zh if which == 0 else 1 - zh

    def at(j, n=1):
        return S.at[pl.ds(2 * j, 2 * n)]

    started = []

    def send(h, num, j, device, n=1, src=None):
        cp = pltpu.make_async_remote_copy(
            src_ref=at(j, n) if src is None else src, dst_ref=at(j, n),
            send_sem=ssem.at[h * HALF + num], recv_sem=rsem.at[h * HALF + num],
            device_id=device, device_id_type=MESH)
        cp.start()
        started.append(cp)

    def recv(h, num, n=1):
        k = h * HALF + num
        pltpu.make_async_copy(S.at[pl.ds(0, 2 * n)], S.at[pl.ds(0, 2 * n)], rsem.at[k]).wait()

    def p2_send(h, piece, which, src=None):
        a, b = pos(h)
        j = sub(h, c, b, wrap(a + OFFS[piece]), zof(which))
        for side in (0, 1):
            send(h, P2 + 4 * piece + 2 * which + side, j, ring(h, 2, side), src=src)

    def encode(j0):
        rows = S[pl.ds(2 * j0, 4)].reshape(256, SZ)
        o = dot_nt(E16[...], rows)
        top, low = o[0:8], o[8:16]
        lane = lax.broadcasted_iota(jnp.int32, (8, 128), 1) % 64
        for half in range(2):
            t = top[:, 128 * half:128 * half + 128]
            u = low[:, 128 * half:128 * half + 128]
            turned = jnp.where(lane < 32, -pltpu.roll(u, 96, 1), pltpu.roll(u, 32, 1))
            W[pl.ds(pl.multiple_of(8 * j0 + 8 * half, 8), 8), :] = t + turned

    def sib_send(h, drow, piece):
        a, b = pos(h)
        j0 = sub(h, c, wrap(b + OFFS[drow]), wrap(a + OFFS[piece]), 0)
        send(h, SIB + 4 * drow + piece, j0, sib, n=2)
        encode(j0)

    def p1_recv(h, which, side):
        recv(h, P1 + 2 * which + side)

    local = []
    for h in (0, 1):
        a, b = pos(h)
        own = sub(h, c, b, a, zh)
        src = src_ref.at[pl.ds(2 * h, 2)]
        send(h, ZX, own, zpart, src=src)
        for side in (0, 1):
            send(h, P1 + side, own, ring(h, 1, side), src=src)
        p2_send(h, 0, 0, src=src)
        cp = pltpu.make_async_copy(src, at(own), lsem.at[h])
        cp.start()
        local.append(cp)

    S[pl.ds(256, 2)] = jnp.zeros((2, 64, SZ), BF)
    cell = cell_ref[...]
    cx, cy, cz = cell // 32, cell // 4 % 8, cell % 4
    cell_in = cx * 32 + cz * 8 + cy
    row = lax.broadcasted_iota(jnp.int32, (256, 256), 0)
    col = lax.broadcasted_iota(jnp.int32, (256, 256), 1)
    row1 = lax.broadcasted_iota(jnp.int32, (256, 1), 0)

    def hot(cond):
        return jnp.where(cond, 1.0, 0.0).astype(BF)

    QI[...] = dot_nt(hot(box_of_input(row1) == col), hot(row == cell_in)).astype(BF)
    QO[...] = dot_nt(hot(4 * (row1 % 64) + row1 // 64 == col), hot(row == cell)).astype(BF)

    in_copies[0].wait()
    pair = ENC2[...].astype(F32)
    E16[...] = jnp.where(lax.rem(bi, 2) == 1, pair[:, 8:16], pair[:, 0:8]).reshape(16, SZ).astype(BF)

    in_copies[1].wait()
    d_i = lax.broadcasted_iota(jnp.int32, (256, 128), 0) % 16
    l_i = lax.broadcasted_iota(jnp.int32, (256, 128), 1)
    ly, lz = l_i // 8, l_i % 8
    close = (((d_i <= 1) | (d_i == 15)) & ((ly <= 1) | (ly == 15)) & ((lz <= 1) | (lz == 7)))
    kept = jnp.where(close, 0.0, KER[...].reshape(256, 128))
    k_hi = kept.astype(BF)
    k_lo = (kept - k_hi.astype(F32)).astype(BF)
    lane512 = lax.broadcasted_iota(jnp.int32, (128, 512), 1)
    take = (lane512 % 64) // 4 * 8 + (lane512 % 4 - lane512 // 128 + 8) % 8
    spread = hot(lax.broadcasted_iota(jnp.int32, (128, 512), 0) == take)
    BASE[...] = (jnp.dot(k_hi, spread, preferred_element_type=F32)
                 + jnp.dot(k_lo, spread, preferred_element_type=F32))

    def build_d(mine):
        col = pl.multiple_of(128 * (zl if mine else 1 - zl), 128)
        dr = DEC[0, :, pl.ds(col, 128)].astype(F32).reshape(64, 1, 8, 128)
        di = DEC[1, :, pl.ds(col, 128)].astype(F32).reshape(64, 1, 8, 128)
        left = jnp.concatenate([dr, -di], axis=1).reshape(1024, 128)
        right = jnp.concatenate([di, dr], axis=1).reshape(1024, 128)
        D[0 if mine else 1] = jnp.concatenate([left, right], axis=1).astype(BF)

    lane = lax.broadcasted_iota(jnp.int32, (8, 128), 1)

    def build_t(k):
        for ri in range(2):
            rows = BASE[pl.ds(pl.multiple_of(32 * k + 16 * ri, 16), 16), :]
            one, two = {}, {}
            for dx in range(-7, 8):
                line = rows[dx % 16:dx % 16 + 1, :]
                one[dx] = [pltpu.roll(jnp.broadcast_to(line[:, 128 * s:128 * s + 128], (8, 128)),
                                      0, 1, stride=4, stride_axis=0) for s in range(4)]
            for d in range(-7, 7):
                two[d] = [jnp.where(lane % 64 < 32, one[d][s], pltpu.roll(one[d + 1][s], 32, 1))
                          for s in range(4)]
            four = {d: [jnp.where(lane < 64, two[d][s], two[d + 2][s]) for s in range(4)]
                    for d in range(-7, 5)}
            wide = jnp.concatenate([
                jnp.concatenate([four[-sx][s], four[4 - sx][s]], axis=1)
                for sx in range(8) for s in range(4)], axis=0)
            hi = wide.astype(BF)
            lo = (wide - hi.astype(F32)).astype(BF)
            for part, val in enumerate((hi, lo)):
                first = dot_nt(QO[...], val).astype(BF)
                TT[k, part, ri] = dot_nt(first, QI[...]).astype(BF)

    def step_t(k):
        lax.fori_loop(k, k + 1, lambda n, _: (build_t(n), 0)[1], 0)

    in_copies[2].wait()
    build_d(False)
    build_d(True)
    for cp in local:
        cp.wait()

    step_t(0)

    for h in (0, 1):
        a, b = pos(h)
        recv(h, ZX)
        other = sub(h, c, b, a, 1 - zh)
        for side in (0, 1):
            send(h, P1 + 2 + side, other, ring(h, 1, side))
        p2_send(h, 0, 1)
        sib_send(h, 0, 0)

    for h in (0, 1):
        a, b = pos(h)
        for side in (0, 1):
            p1_recv(h, 0, side)
        send(h, F1, sub(h, c, b, wrap(a - 1), zh), ring(h, 1, 0))
        p2_send(h, 1, 0)
        p2_send(h, 2, 0)

    step_t(1)

    for h in (0, 1):
        a, b = pos(h)
        for side in (0, 1):
            recv(h, P2 + side)
        send(h, F2, sub(h, c, wrap(b - 1), a, zh), ring(h, 2, 0))

    step_t(2)

    for h in (0, 1):
        a, b = pos(h)
        for side in (0, 1):
            p1_recv(h, 1, side)
        send(h, F1 + 1, sub(h, c, b, wrap(a + 1), 1 - zh), ring(h, 1, 1))
        p2_send(h, 1, 1)
        p2_send(h, 2, 1)
        sib_send(h, 0, 1)
        sib_send(h, 0, 2)

    step_t(3)

    for h in (0, 1):
        a, b = pos(h)
        for side in (0, 1):
            recv(h, P2 + 2 + side)
        send(h, F2 + 1, sub(h, c, wrap(b + 1), a, 1 - zh), ring(h, 2, 1))
        sib_send(h, 1, 0)
        sib_send(h, 2, 0)

    step_t(4)

    for h in (0, 1):
        for side in (0, 1):
            recv(h, F1 + side)
        p2_send(h, 3, 0)
        p2_send(h, 3, 1)
        sib_send(h, 0, 3)

    step_t(5)

    def relay(h, piece):
        a, b = pos(h)
        p1 = wrap(a + OFFS[piece])
        for which in (0, 1):
            for side in (0, 1):
                recv(h, P2 + 4 * piece + 2 * which + side)
            if which == 0:
                send(h, F2 + 2 * piece, sub(h, c, wrap(b - 1), p1, zh), ring(h, 2, 0))
            else:
                send(h, F2 + 2 * piece + 1, sub(h, c, wrap(b + 1), p1, 1 - zh), ring(h, 2, 1))
        sib_send(h, 1, piece)
        sib_send(h, 2, piece)

    for piece in (1, 2):
        for h in (0, 1):
            relay(h, piece)
        step_t(5 + piece)
    for h in (0, 1):
        relay(h, 3)

    for piece in range(4):
        for h in (0, 1):
            for side in (0, 1):
                recv(h, F2 + 2 * piece + side)
            sib_send(h, 3, piece)

    for drow in range(4):
        for piece in range(4):
            for h in (0, 1):
                a, b = pos(h)
                recv(h, SIB + 4 * drow + piece, n=2)
                encode(sub(h, 1 - c, wrap(b + OFFS[drow]), wrap(a + OFFS[piece]), 0))

    pl.semaphore_signal(ready, inc=1, device_id=partner, device_id_type=MESH)
    for cp in started:
        cp.wait_send()

    lane64 = lax.broadcasted_iota(jnp.int32, (256, 64), 1)
    quarter = lax.broadcasted_iota(jnp.int32, (64, 128), 1) // 32

    def translate(k, _):
        v = W[pl.ds(k, 128, stride=8), :]
        e = jnp.concatenate([v[:, 0:64], v[:, 64:128]], axis=0)
        hi = e.astype(BF)
        lo = (e - hi.astype(F32)).astype(BF)
        t_hi = TT[k, 0].reshape(512, 256)
        t_lo = TT[k, 1].reshape(512, 256)
        nn = (((1,), (0,)), ((), ()))
        f = lax.dot_general(t_hi, hi, nn, preferred_element_type=F32)
        f = f + lax.dot_general(t_hi, lo, nn, preferred_element_type=F32)
        f = f + lax.dot_general(t_lo, hi, nn, preferred_element_type=F32)
        fr, fi = f[0:256], f[256:512]
        swapped = jnp.concatenate([fi[:, 32:64], fi[:, 0:32]], axis=1)
        far = fr + jnp.where(lane64 < 32, -swapped, swapped)
        far = jnp.concatenate([far, far], axis=1)
        far_sw = pltpu.roll(far, 32, 1)
        for ri in range(2):
            val = None
            for q in range(4):
                use = far if (q - ri) % 2 == 0 else far_sw
                block = use[64 * q:64 * q + 64]
                val = block if val is None else jnp.where(quarter == q, block, val)
            V[pl.ds(8 * ri + k, 64, stride=16), :] = val
        return 0

    lax.fori_loop(0, KD, translate, 0)
    SEND[...] = V[...].astype(BF).reshape(64, 16, 128)
    R[pl.ds(bi, 1)] = SEND[pl.ds(bi, 1)]

    def scatter(t, _):
        dst = lax.rem(bi + t, NB)
        pltpu.make_async_remote_copy(
            src_ref=SEND.at[dst], dst_ref=R.at[bi], send_sem=a2s.at[0], recv_sem=a2r.at[0],
            device_id=(dst, zl), device_id_type=MESH).start()
        return 0

    pl.semaphore_wait(ready, 1)
    lax.fori_loop(1, NB, scatter, 0)

    def near_box(q, _):
        blocks = NBV[q]
        xs = jnp.concatenate(
            [S[jnp.where(mask_ref[q, s] == 1, slot_of_box(list_ref[q, s]), 256)]
             for s in range(SLOTS)], axis=1)
        bs = jnp.concatenate([blocks[s] for s in range(SLOTS)], axis=1)
        n = dot_nt(xs, bs)
        NEAR[q, 0] = n[0:32, 0:256] - n[32:64, 256:512]
        NEAR[q, 1] = n[32:64, 0:256] + n[0:32, 256:512]
        return 0

    for cp in nb_copies:
        cp.wait()
    lax.fori_loop(0, PER, near_box, 0)

    mine = pl.multiple_of(128 * zl, 128)
    theirs = pl.multiple_of(128 * (1 - zl), 128)
    NS[...] = NEAR[:, :, :, pl.ds(theirs, 128)]
    near_out = pltpu.make_async_remote_copy(
        src_ref=NS, dst_ref=NR, send_sem=pss.at[0], recv_sem=psr.at[0],
        device_id=partner, device_id_type=MESH)
    near_out.start()

    whole = R.at[pl.ds(0, NB - 1)]
    pltpu.make_async_copy(whole, whole, a2r.at[0]).wait()
    got = R[...].reshape(1024, 128)

    def decode(which):
        return lax.dot_general(got, D[which], (((0,), (0,)), ((), ())), preferred_element_type=F32)

    FS[...] = decode(1).astype(BF)
    far_out = pltpu.make_async_remote_copy(
        src_ref=FS, dst_ref=FR, send_sem=pss.at[1], recv_sem=psr.at[1],
        device_id=partner, device_id_type=MESH)
    far_out.start()
    far = decode(0)
    near_out.wait()
    for q in range(4):
        for ro in range(2):
            out_ref[q, ro] = (far[32 * q:32 * q + 32, 128 * ro:128 * ro + 128]
                              + NEAR[q, ro, :, pl.ds(mine, 128)] + NR[q, ro])
    sent = SEND.at[pl.ds(0, NB - 1)]
    pltpu.make_async_copy(sent, sent, a2s.at[0]).wait()
    far_out.wait()
    for q in range(4):
        for ro in range(2):
            out_ref[q, ro] += FR[32 * q:32 * q + 32, 128 * ro:128 * ro + 128].astype(F32)


def on_device(sources, encode, kernel, decode, near_blocks, near_list, near_mask, box_cell):
    smem = pl.BlockSpec(memory_space=pltpu.SMEM)
    hbm = pl.BlockSpec(memory_space=pl.ANY)
    vm = pl.BlockSpec(memory_space=pltpu.VMEM)
    n_sem = 2 * HALF
    return pl.pallas_call(
        body,
        out_shape=jax.ShapeDtypeStruct((PER, 2, RHS, 128), F32),
        in_specs=[smem, smem, vm, hbm, hbm, hbm, hbm, hbm],
        out_specs=vm,
        scratch_shapes=[
            pltpu.VMEM((258, 64, SZ), BF),
            pltpu.VMEM((1024, 128), F32),
            pltpu.VMEM((KD, 2, 2, 256, 256), BF),
            pltpu.VMEM((2, 1024, 256), BF),
            pltpu.VMEM((1024, 128), F32),
            pltpu.VMEM((NB, 16, 128), BF),
            pltpu.VMEM((NB, 16, 128), BF),
            pltpu.VMEM((PER, SLOTS, 512, SZ), BF),
            pltpu.VMEM((PER, 2, RHS, SZ), F32),
            pltpu.VMEM((PER, 2, RHS, 128), F32),
            pltpu.VMEM((PER, 2, RHS, 128), F32),
            pltpu.VMEM((128, 256), BF),
            pltpu.VMEM((128, 256), BF),
            pltpu.VMEM((256, 256), BF),
            pltpu.VMEM((256, 256), BF),
            pltpu.VMEM((256, 512), F32),
            pltpu.VMEM((2, 16, SZ), BF),
            pltpu.VMEM((16, SZ), BF),
            pltpu.VMEM((KD, 2, 16, 128), F32),
            pltpu.VMEM((2, 512, SZ), BF),
            pltpu.SemaphoreType.DMA((n_sem,)),
            pltpu.SemaphoreType.DMA((n_sem,)),
            pltpu.SemaphoreType.DMA((2,)),
            pltpu.SemaphoreType.DMA((PER,)),
            pltpu.SemaphoreType.DMA((3,)),
            pltpu.SemaphoreType.DMA((1,)),
            pltpu.SemaphoreType.DMA((1,)),
            pltpu.SemaphoreType.DMA((2,)),
            pltpu.SemaphoreType.DMA((2,)),
            pltpu.SemaphoreType.REGULAR,
        ],
        compiler_params=pltpu.CompilerParams(
            collective_id=0, has_side_effects=True, vmem_limit_bytes=56 * 2**20),
        name="fmm",
    )(near_list, near_mask, box_cell.reshape(1, 256), sources.reshape(PER, 64, SZ), encode, kernel,
      decode, near_blocks.reshape(PER, SLOTS, 512, SZ))


def solution(mesh):
    in_specs = (
        P("box", None, None, None),
        P(None, "dir", None),
        P(("dir", "box"), None, None, None),
        P(None, "dir", None),
        P("box", "dir", None, None, None),
        P("box", "dir"),
        P("box", "dir"),
        P(),
    )
    return jax.shard_map(
        on_device, mesh=mesh, in_specs=in_specs, out_specs=P("box", None, None, "dir"),
        check_vma=False)
```

```python
import jax
import jax.numpy as jnp
from jax import lax
from jax.experimental import pallas as pl
from jax.experimental.pallas import tpu as pltpu
from jax.sharding import PartitionSpec as P

MESH = pl.DeviceIdType.MESH
BF = jnp.bfloat16
F32 = jnp.float32

NB = 64
PER = 4
KD = 8
RHS = 32
SLOTS = 14
SZ = 256

ZX = 0
P1 = 1
F1 = 5
P2 = 7
F2 = 23
SIB = 31
PX = 47
HALF = 59
OFFS = (0, -1, 1, 2)


def box_of_input(i):
    w, j = i // 128, i % 128
    h, c, p2, p1, z = j // 64, j // 32 % 2, j // 8 % 4, j // 2 % 4, j % 2
    y = jnp.where(h == 0, p2, p1)
    x = jnp.where(h == 0, p1, p2)
    return (((y * 2 + z) * 4 + x) * 2 + c) * 4 + 2 * h + w


def slot_of_box(v):
    w, h, c = lax.rem(v, 2), lax.rem(v // 2, 2), lax.rem(v // 4, 2)
    x, z, y = lax.rem(v // 8, 4), lax.rem(v // 32, 2), v // 64
    first = 8 * y + 2 * x
    second = 8 * x + 2 * y
    return 2 * (h * 64 + c * 32 + jnp.where(h == 1, second, first) + z) + w


def dot_nt(a, b):
    return lax.dot_general(a, b, (((1,), (1,)), ((), ())), preferred_element_type=F32)


def body(list_ref, mask_ref, cell_ref, src_ref, enc_hbm, ker_hbm, dec_hbm, nb_hbm, out_ref,
         S, W, TT, D, V, SEND, R, NBV, NEAR, NS, NR, FS, FR, QI, QO, BASE, ENC2, E16, KER, DEC,
         ssem, rsem, lsem, nsem, isem, a2s, a2r, pss, psr, ready):
    bi = lax.axis_index("box")
    zl = lax.axis_index("dir")
    c = lax.rem(bi, 2)
    x = lax.rem(bi // 2, 4)
    zh = lax.rem(bi // 8, 2)
    y = bi // 16

    def dev(y_, zh_, x_, c_):
        return ((y_ * 2 + zh_) * 4 + x_) * 2 + c_

    def wrap(v):
        return lax.rem(v + 8, 4)

    zpart = (dev(y, 1 - zh, x, c), 1 - zl)
    sib = (dev(y, zh, x, 1 - c), zl)
    partner = (bi, 1 - zl)

    right, left = (dev(y, zh, wrap(x + 1), c), zl), (dev(y, zh, wrap(x - 1), c), zl)
    up, down = (dev(wrap(y + 1), zh, x, c), zl), (dev(wrap(y - 1), zh, x, c), zl)
    bar = pltpu.get_barrier_semaphore()
    for other in (right, left, up, down, zpart, sib, partner):
        pl.semaphore_signal(bar, inc=1, device_id=other, device_id_type=MESH)

    in_copies = [
        pltpu.make_async_copy(enc_hbm.at[:, pl.ds(pl.multiple_of(16 * (bi // 2), 16), 16), :], ENC2, isem.at[0]),
        pltpu.make_async_copy(ker_hbm, KER, isem.at[1]),
        pltpu.make_async_copy(dec_hbm, DEC, isem.at[2])]
    for cp in in_copies:
        cp.start()
    nb_copies = [pltpu.make_async_copy(nb_hbm.at[q], NBV.at[q], nsem.at[q]) for q in range(PER)]
    for cp in nb_copies:
        cp.start()
    pl.semaphore_wait(bar, 7)

    def pos(h):
        return (x, y) if h == 0 else (y, x)

    def ring(h, level, side):
        step = 1 if side == 0 else -1
        along_x = (h == 0) == (level == 1)
        if along_x:
            return (dev(y, zh, wrap(x + step), c), zl)
        return (dev(wrap(y + step), zh, x, c), zl)

    def sub(h, c_, p2, p1, z):
        return h * 64 + c_ * 32 + p2 * 8 + p1 * 2 + z

    def zof(which):
        return zh if which == 0 else 1 - zh

    def at(j, n=1):
        return S.at[pl.ds(2 * j, 2 * n)]

    started = []

    def copy(h, num, src, dst, device):
        cp = pltpu.make_async_remote_copy(
            src_ref=src, dst_ref=dst,
            send_sem=ssem.at[h * HALF + num], recv_sem=rsem.at[h * HALF + num],
            device_id=device, device_id_type=MESH)
        cp.start()
        started.append(cp)

    def send(h, num, j, device, n=1, src=None):
        copy(h, num, at(j, n) if src is None else src, at(j, n), device)

    def send_box(h, num, j, device, src=None):
        one = S.at[pl.ds(2 * j + zl, 1)]
        copy(h, num, one if src is None else src, one, device)

    def recv(h, num, boxes=2):
        k = h * HALF + num
        pltpu.make_async_copy(S.at[pl.ds(0, boxes)], S.at[pl.ds(0, boxes)], rsem.at[k]).wait()

    def spot(h, drow, piece, which):
        a, b = pos(h)
        return sub(h, c, wrap(b + OFFS[drow]), wrap(a + OFFS[piece]), zof(which))

    def p2_send(h, piece, which, src=None):
        j = spot(h, 0, piece, which)
        for side in (0, 1):
            num = P2 + 4 * piece + 2 * which + side
            if piece < 2:
                send_box(h, num, j, ring(h, 2, side), src)
            else:
                send(h, num, j, ring(h, 2, side), src=src)

    def p2_recv(h, piece, which):
        for side in (0, 1):
            recv(h, P2 + 4 * piece + 2 * which + side, 1 if piece < 2 else 2)

    def f2_send(h, piece, which):
        j = spot(h, 1 if which == 0 else 2, piece, which)
        num = F2 + 2 * piece + which
        if piece < 2:
            send_box(h, num, j, ring(h, 2, which))
        else:
            send(h, num, j, ring(h, 2, which))

    def f2_recv(h, piece):
        for side in (0, 1):
            recv(h, F2 + 2 * piece + side, 1 if piece < 2 else 2)

    def px_send(h, piece, drow, which):
        send_box(h, PX + 6 * piece + 2 * (drow - 1) + which, spot(h, drow, piece, which), partner)

    def px_recv(h, piece, drow):
        for which in (0, 1):
            recv(h, PX + 6 * piece + 2 * (drow - 1) + which, 1)

    def encode(j0):
        rows = S[pl.ds(2 * j0, 4)].reshape(256, SZ)
        o = dot_nt(E16[...], rows)
        top, low = o[0:8], o[8:16]
        lane = lax.broadcasted_iota(jnp.int32, (8, 128), 1) % 64
        for half in range(2):
            t = top[:, 128 * half:128 * half + 128]
            u = low[:, 128 * half:128 * half + 128]
            turned = jnp.where(lane < 32, -pltpu.roll(u, 96, 1), pltpu.roll(u, 32, 1))
            W[pl.ds(pl.multiple_of(8 * j0 + 8 * half, 8), 8), :] = t + turned

    def pair(h, c_, drow, piece):
        a, b = pos(h)
        return sub(h, c_, wrap(b + OFFS[drow]), wrap(a + OFFS[piece]), 0)

    earlier = []

    def finish(pairs):
        for h, drow, piece in pairs:
            send(h, SIB + 4 * drow + piece, pair(h, c, drow, piece), sib, n=2)
        for h, drow, piece in pairs:
            encode(pair(h, c, drow, piece))
        for h, drow, piece in earlier:
            recv(h, SIB + 4 * drow + piece, 4)
        for h, drow, piece in earlier:
            encode(pair(h, 1 - c, drow, piece))
        earlier[:] = pairs

    local = []
    for h in (0, 1):
        own = spot(h, 0, 0, 0)
        src = src_ref.at[pl.ds(2 * h, 2)]
        for side in (0, 1):
            send(h, P1 + side, own, ring(h, 1, side), src=src)
        send(h, ZX, own, zpart, src=src)
        cp = pltpu.make_async_copy(src, at(own), lsem.at[h])
        cp.start()
        local.append(cp)
    for h in (0, 1):
        p2_send(h, 0, 0, src=src_ref.at[pl.ds(2 * h + zl, 1)])

    S[pl.ds(256, 2)] = jnp.zeros((2, 64, SZ), BF)
    cell = cell_ref[...]
    cx, cy, cz = cell // 32, cell // 4 % 8, cell % 4
    cell_in = cx * 32 + cz * 8 + cy
    row = lax.broadcasted_iota(jnp.int32, (256, 256), 0)
    col = lax.broadcasted_iota(jnp.int32, (256, 256), 1)
    row1 = lax.broadcasted_iota(jnp.int32, (256, 1), 0)

    def hot(cond):
        return jnp.where(cond, 1.0, 0.0).astype(BF)

    QI[...] = dot_nt(hot(box_of_input(row1) == col), hot(row == cell_in)).astype(BF)
    QO[...] = dot_nt(hot(4 * (row1 % 64) + row1 // 64 == col), hot(row == cell)).astype(BF)

    in_copies[0].wait()
    two_rows = ENC2[...].astype(F32)
    E16[...] = jnp.where(lax.rem(bi, 2) == 1, two_rows[:, 8:16], two_rows[:, 0:8]).reshape(16, SZ).astype(BF)

    in_copies[1].wait()
    d_i = lax.broadcasted_iota(jnp.int32, (256, 128), 0) % 16
    l_i = lax.broadcasted_iota(jnp.int32, (256, 128), 1)
    ly, lz = l_i // 8, l_i % 8
    close = (((d_i <= 1) | (d_i == 15)) & ((ly <= 1) | (ly == 15)) & ((lz <= 1) | (lz == 7)))
    kept = jnp.where(close, 0.0, KER[...].reshape(256, 128))
    k_hi = kept.astype(BF)
    k_lo = (kept - k_hi.astype(F32)).astype(BF)
    lane512 = lax.broadcasted_iota(jnp.int32, (128, 512), 1)
    take = (lane512 % 64) // 4 * 8 + (lane512 % 4 - lane512 // 128 + 8) % 8
    spread = hot(lax.broadcasted_iota(jnp.int32, (128, 512), 0) == take)
    BASE[...] = (jnp.dot(k_hi, spread, preferred_element_type=F32)
                 + jnp.dot(k_lo, spread, preferred_element_type=F32))

    def build_d(mine):
        col = pl.multiple_of(128 * (zl if mine else 1 - zl), 128)
        dr = DEC[0, :, pl.ds(col, 128)].astype(F32).reshape(64, 1, 8, 128)
        di = DEC[1, :, pl.ds(col, 128)].astype(F32).reshape(64, 1, 8, 128)
        left = jnp.concatenate([dr, -di], axis=1).reshape(1024, 128)
        right = jnp.concatenate([di, dr], axis=1).reshape(1024, 128)
        D[0 if mine else 1] = jnp.concatenate([left, right], axis=1).astype(BF)

    lane = lax.broadcasted_iota(jnp.int32, (8, 128), 1)

    def build_t(k):
        for ri in range(2):
            rows = BASE[pl.ds(pl.multiple_of(32 * k + 16 * ri, 16), 16), :]
            one, two = {}, {}
            for dx in range(-7, 8):
                line = rows[dx % 16:dx % 16 + 1, :]
                one[dx] = [pltpu.roll(jnp.broadcast_to(line[:, 128 * s:128 * s + 128], (8, 128)),
                                      0, 1, stride=4, stride_axis=0) for s in range(4)]
            for d in range(-7, 7):
                two[d] = [jnp.where(lane % 64 < 32, one[d][s], pltpu.roll(one[d + 1][s], 32, 1))
                          for s in range(4)]
            four = {d: [jnp.where(lane < 64, two[d][s], two[d + 2][s]) for s in range(4)]
                    for d in range(-7, 5)}
            wide = jnp.concatenate([
                jnp.concatenate([four[-sx][s], four[4 - sx][s]], axis=1)
                for sx in range(8) for s in range(4)], axis=0)
            hi = wide.astype(BF)
            lo = (wide - hi.astype(F32)).astype(BF)
            for part, val in enumerate((hi, lo)):
                first = dot_nt(QO[...], val).astype(BF)
                TT[k, part, ri] = dot_nt(first, QI[...]).astype(BF)

    def step_t(k):
        lax.fori_loop(k, k + 1, lambda n, _: (build_t(n), 0)[1], 0)

    def step_t(k):
        lax.fori_loop(k, k + 1, lambda n, _: (build_t(n), 0)[1], 0)

    for cp in local:
        cp.wait()
    both = (0, 1)

    for h in both:
        for side in both:
            recv(h, P1 + side)
        send(h, F1, spot(h, 0, 1, 0), ring(h, 1, 0))
        p2_send(h, 1, 0)
        p2_send(h, 2, 0)
    for h in both:
        recv(h, ZX)
        for side in both:
            send(h, P1 + 2 + side, spot(h, 0, 0, 1), ring(h, 1, side))
        p2_send(h, 0, 1)
    for h in both:
        p2_recv(h, 0, 0)
        f2_send(h, 0, 0)
        px_send(h, 0, 1, 0)
        px_send(h, 0, 2, 0)
    finish([(h, 0, 0) for h in both])
    step_t(0)
    for h in both:
        for side in both:
            recv(h, P1 + 2 + side)
        send(h, F1 + 1, spot(h, 0, 2, 1), ring(h, 1, 1))
        p2_send(h, 1, 1)
        p2_send(h, 2, 1)
    finish([(h, 0, piece) for piece in (1, 2) for h in both])
    for h in both:
        p2_recv(h, 0, 1)
        f2_send(h, 0, 1)
        px_send(h, 0, 1, 1)
        px_send(h, 0, 2, 1)
    step_t(1)
    for h in both:
        for side in both:
            recv(h, F1 + side)
        p2_send(h, 3, 0)
        p2_send(h, 3, 1)
    finish([(h, 0, 3) for h in both])
    step_t(2)
    for h in both:
        p2_recv(h, 1, 0)
        f2_send(h, 1, 0)
        px_send(h, 1, 1, 0)
        px_send(h, 1, 2, 0)
    for h in both:
        for drow in (1, 2):
            px_recv(h, 0, drow)
    finish([(h, drow, 0) for drow in (1, 2) for h in both])
    step_t(3)
    for h in both:
        p2_recv(h, 1, 1)
        f2_send(h, 1, 1)
        px_send(h, 1, 1, 1)
        px_send(h, 1, 2, 1)
    for h in both:
        f2_recv(h, 0)
        px_send(h, 0, 3, 0)
        px_send(h, 0, 3, 1)
    step_t(4)
    for h in both:
        for which in both:
            p2_recv(h, 2, which)
            f2_send(h, 2, which)
    finish([(h, drow, 2) for drow in (1, 2) for h in both])
    step_t(5)
    for h in both:
        f2_recv(h, 1)
        px_send(h, 1, 3, 0)
        px_send(h, 1, 3, 1)
    for h in both:
        for drow in (1, 2):
            px_recv(h, 1, drow)
        px_recv(h, 0, 3)
    finish([(h, drow, 1) for drow in (1, 2) for h in both] + [(h, 3, 0) for h in both])
    step_t(6)
    for h in both:
        for which in both:
            p2_recv(h, 3, which)
            f2_send(h, 3, which)
    finish([(h, drow, 3) for drow in (1, 2) for h in both])
    step_t(7)
    in_copies[2].wait()
    build_d(False)
    build_d(True)
    for h in both:
        f2_recv(h, 2)
        px_recv(h, 1, 3)
    finish([(h, 3, piece) for piece in (1, 2) for h in both])
    for h in both:
        f2_recv(h, 3)
    finish([(h, 3, 3) for h in both])
    finish([])

    pl.semaphore_signal(ready, inc=1, device_id=partner, device_id_type=MESH)
    lane64 = lax.broadcasted_iota(jnp.int32, (256, 64), 1)
    quarter = lax.broadcasted_iota(jnp.int32, (64, 128), 1) // 32

    def translate(k, _):
        v = W[pl.ds(k, 128, stride=8), :]
        e = jnp.concatenate([v[:, 0:64], v[:, 64:128]], axis=0)
        hi = e.astype(BF)
        lo = (e - hi.astype(F32)).astype(BF)
        t_hi = TT[k, 0].reshape(512, 256)
        t_lo = TT[k, 1].reshape(512, 256)
        nn = (((1,), (0,)), ((), ()))
        wide = lax.dot_general(t_hi, jnp.concatenate([hi, lo], axis=1), nn, preferred_element_type=F32)
        f = wide[:, 0:64] + wide[:, 64:128]
        f = f + lax.dot_general(t_lo, hi, nn, preferred_element_type=F32)
        fr, fi = f[0:256], f[256:512]
        swapped = jnp.concatenate([fi[:, 32:64], fi[:, 0:32]], axis=1)
        far = fr + jnp.where(lane64 < 32, -swapped, swapped)
        far = jnp.concatenate([far, far], axis=1)
        far_sw = pltpu.roll(far, 32, 1)
        for ri in range(2):
            val = None
            for q in range(4):
                use = far if (q - ri) % 2 == 0 else far_sw
                block = use[64 * q:64 * q + 64]
                val = block if val is None else jnp.where(quarter == q, block, val)
            V[pl.ds(8 * ri + k, 64, stride=16), :] = val
        return 0

    lax.fori_loop(0, KD, translate, 0, unroll=2)
    SEND[...] = V[...].astype(BF).reshape(64, 16, 128)
    R[pl.ds(bi, 1)] = SEND[pl.ds(bi, 1)]

    def scatter(t, _):
        dst = lax.rem(bi + t, NB)
        pltpu.make_async_remote_copy(
            src_ref=SEND.at[dst], dst_ref=R.at[bi], send_sem=a2s.at[0], recv_sem=a2r.at[0],
            device_id=(dst, zl), device_id_type=MESH).start()
        return 0

    pl.semaphore_wait(ready, 1)
    lax.fori_loop(1, NB, scatter, 0)

    def near_box(q, _):
        blocks = NBV[q]
        xs = jnp.concatenate(
            [S[jnp.where(mask_ref[q, s] == 1, slot_of_box(list_ref[q, s]), 256)]
             for s in range(SLOTS)], axis=1)
        bs = jnp.concatenate([blocks[s] for s in range(SLOTS)], axis=1)
        n = dot_nt(xs, bs)
        NEAR[q, 0] = n[0:32, 0:256] - n[32:64, 256:512]
        NEAR[q, 1] = n[32:64, 0:256] + n[0:32, 256:512]
        return 0

    for cp in nb_copies:
        cp.wait()
    lax.fori_loop(0, PER, near_box, 0)

    mine = pl.multiple_of(128 * zl, 128)
    theirs = pl.multiple_of(128 * (1 - zl), 128)
    NS[...] = NEAR[:, :, :, pl.ds(theirs, 128)]
    near_out = pltpu.make_async_remote_copy(
        src_ref=NS, dst_ref=NR, send_sem=pss.at[0], recv_sem=psr.at[0],
        device_id=partner, device_id_type=MESH)
    near_out.start()

    whole = R.at[pl.ds(0, NB - 1)]
    pltpu.make_async_copy(whole, whole, a2r.at[0]).wait()
    got = R[...].reshape(1024, 128)

    def decode(which):
        return lax.dot_general(got, D[which], (((0,), (0,)), ((), ())), preferred_element_type=F32)

    FS[...] = decode(1).astype(BF)
    far_out = pltpu.make_async_remote_copy(
        src_ref=FS, dst_ref=FR, send_sem=pss.at[1], recv_sem=psr.at[1],
        device_id=partner, device_id_type=MESH)
    far_out.start()
    far = decode(0)
    near_out.wait()
    for q in range(4):
        for ro in range(2):
            out_ref[q, ro] = (far[32 * q:32 * q + 32, 128 * ro:128 * ro + 128]
                              + NEAR[q, ro, :, pl.ds(mine, 128)] + NR[q, ro])
    sent = SEND.at[pl.ds(0, NB - 1)]
    pltpu.make_async_copy(sent, sent, a2s.at[0]).wait()
    for cp in started:
        cp.wait_send()
    far_out.wait()
    for q in range(4):
        for ro in range(2):
            out_ref[q, ro] += FR[32 * q:32 * q + 32, 128 * ro:128 * ro + 128].astype(F32)


def on_device(sources, encode, kernel, decode, near_blocks, near_list, near_mask, box_cell):
    smem = pl.BlockSpec(memory_space=pltpu.SMEM)
    hbm = pl.BlockSpec(memory_space=pl.ANY)
    vm = pl.BlockSpec(memory_space=pltpu.VMEM)
    n_sem = 2 * HALF
    return pl.pallas_call(
        body,
        out_shape=jax.ShapeDtypeStruct((PER, 2, RHS, 128), F32),
        in_specs=[smem, smem, vm, hbm, hbm, hbm, hbm, hbm],
        out_specs=vm,
        scratch_shapes=[
            pltpu.VMEM((258, 64, SZ), BF),
            pltpu.VMEM((1024, 128), F32),
            pltpu.VMEM((KD, 2, 2, 256, 256), BF),
            pltpu.VMEM((2, 1024, 256), BF),
            pltpu.VMEM((1024, 128), F32),
            pltpu.VMEM((NB, 16, 128), BF),
            pltpu.VMEM((NB, 16, 128), BF),
            pltpu.VMEM((PER, SLOTS, 512, SZ), BF),
            pltpu.VMEM((PER, 2, RHS, SZ), F32),
            pltpu.VMEM((PER, 2, RHS, 128), F32),
            pltpu.VMEM((PER, 2, RHS, 128), F32),
            pltpu.VMEM((128, 256), BF),
            pltpu.VMEM((128, 256), BF),
            pltpu.VMEM((256, 256), BF),
            pltpu.VMEM((256, 256), BF),
            pltpu.VMEM((256, 512), F32),
            pltpu.VMEM((2, 16, SZ), BF),
            pltpu.VMEM((16, SZ), BF),
            pltpu.VMEM((KD, 2, 16, 128), F32),
            pltpu.VMEM((2, 512, SZ), BF),
            pltpu.SemaphoreType.DMA((n_sem,)),
            pltpu.SemaphoreType.DMA((n_sem,)),
            pltpu.SemaphoreType.DMA((2,)),
            pltpu.SemaphoreType.DMA((PER,)),
            pltpu.SemaphoreType.DMA((3,)),
            pltpu.SemaphoreType.DMA((1,)),
            pltpu.SemaphoreType.DMA((1,)),
            pltpu.SemaphoreType.DMA((2,)),
            pltpu.SemaphoreType.DMA((2,)),
            pltpu.SemaphoreType.REGULAR,
        ],
        compiler_params=pltpu.CompilerParams(
            collective_id=0, has_side_effects=True, vmem_limit_bytes=56 * 2**20),
        name="fmm",
    )(near_list, near_mask, box_cell.reshape(1, 256), sources.reshape(PER, 64, SZ), encode, kernel,
      decode, near_blocks.reshape(PER, SLOTS, 512, SZ))


def solution(mesh):
    in_specs = (
        P("box", None, None, None),
        P(None, "dir", None),
        P(("dir", "box"), None, None, None),
        P(None, "dir", None),
        P("box", "dir", None, None, None),
        P("box", "dir"),
        P("box", "dir"),
        P(),
    )
    return jax.shard_map(
        on_device, mesh=mesh, in_specs=in_specs, out_specs=P("box", None, None, "dir"),
        check_vma=False)
```

```python
import jax
import jax.numpy as jnp
from jax import lax
from jax.experimental import pallas as pl
from jax.experimental.pallas import tpu as pltpu
from jax.sharding import PartitionSpec as P

MESH = pl.DeviceIdType.MESH
BF = jnp.bfloat16
F32 = jnp.float32

NB = 64
PER = 4
KD = 8
RHS = 32
SLOTS = 14
SZ = 256

ZX = 0
P1 = 1
F1 = 5
P2 = 7
F2 = 23
SIB = 31
PX = 47
HALF = 59
OFFS = (0, -1, 1, 2)


def box_of_input(i):
    w, j = i // 128, i % 128
    h, c, p2, p1, z = j // 64, j // 32 % 2, j // 8 % 4, j // 2 % 4, j % 2
    y = jnp.where(h == 0, p2, p1)
    x = jnp.where(h == 0, p1, p2)
    return (((y * 2 + z) * 4 + x) * 2 + c) * 4 + 2 * h + w


def slot_of_box(v):
    w, h, c = lax.rem(v, 2), lax.rem(v // 2, 2), lax.rem(v // 4, 2)
    x, z, y = lax.rem(v // 8, 4), lax.rem(v // 32, 2), v // 64
    first = 8 * y + 2 * x
    second = 8 * x + 2 * y
    return 2 * (h * 64 + c * 32 + jnp.where(h == 1, second, first) + z) + w


def dot_nt(a, b):
    return lax.dot_general(a, b, (((1,), (1,)), ((), ())), preferred_element_type=F32)


def body(list_ref, mask_ref, cell_ref, src_ref, enc_hbm, ker_hbm, dec_hbm, nb_hbm, out_ref,
         S, W, TT, D, V, SEND, R, NBV, NEAR, NS, NR, FS, FR, QI, QO, BASE, ENC2, E16, KER, DEC,
         ssem, rsem, lsem, nsem, isem, a2s, a2r, pss, psr, ready):
    bi = lax.axis_index("box")
    zl = lax.axis_index("dir")
    c = lax.rem(bi, 2)
    x = lax.rem(bi // 2, 4)
    zh = lax.rem(bi // 8, 2)
    y = bi // 16

    def dev(y_, zh_, x_, c_):
        return ((y_ * 2 + zh_) * 4 + x_) * 2 + c_

    def wrap(v):
        return lax.rem(v + 8, 4)

    zpart = (dev(y, 1 - zh, x, c), 1 - zl)
    sib = (dev(y, zh, x, 1 - c), zl)
    partner = (bi, 1 - zl)

    right, left = (dev(y, zh, wrap(x + 1), c), zl), (dev(y, zh, wrap(x - 1), c), zl)
    up, down = (dev(wrap(y + 1), zh, x, c), zl), (dev(wrap(y - 1), zh, x, c), zl)
    bar = pltpu.get_barrier_semaphore()
    for other in (right, left, up, down, zpart, sib, partner):
        pl.semaphore_signal(bar, inc=1, device_id=other, device_id_type=MESH)

    in_copies = [
        pltpu.make_async_copy(enc_hbm.at[:, pl.ds(pl.multiple_of(16 * (bi // 2), 16), 16), :], ENC2, isem.at[0]),
        pltpu.make_async_copy(ker_hbm, KER, isem.at[1]),
        pltpu.make_async_copy(dec_hbm, DEC, isem.at[2])]
    for cp in in_copies:
        cp.start()
    nb_copies = [pltpu.make_async_copy(nb_hbm.at[q], NBV.at[q], nsem.at[q]) for q in range(PER)]
    for cp in nb_copies:
        cp.start()
    pl.semaphore_wait(bar, 7)

    def pos(h):
        return (x, y) if h == 0 else (y, x)

    def ring(h, level, side):
        step = 1 if side == 0 else -1
        along_x = (h == 0) == (level == 1)
        if along_x:
            return (dev(y, zh, wrap(x + step), c), zl)
        return (dev(wrap(y + step), zh, x, c), zl)

    def sub(h, c_, p2, p1, z):
        return h * 64 + c_ * 32 + p2 * 8 + p1 * 2 + z

    def zof(which):
        return zh if which == 0 else 1 - zh

    def at(j, n=1):
        return S.at[pl.ds(2 * j, 2 * n)]

    started = []

    def copy(h, num, src, dst, device):
        cp = pltpu.make_async_remote_copy(
            src_ref=src, dst_ref=dst,
            send_sem=ssem.at[h * HALF + num], recv_sem=rsem.at[h * HALF + num],
            device_id=device, device_id_type=MESH)
        cp.start()
        started.append(cp)

    def send(h, num, j, device, n=1, src=None):
        copy(h, num, at(j, n) if src is None else src, at(j, n), device)

    def send_box(h, num, j, device, src=None):
        one = S.at[pl.ds(2 * j + zl, 1)]
        copy(h, num, one if src is None else src, one, device)

    def recv(h, num, boxes=2):
        k = h * HALF + num
        pltpu.make_async_copy(S.at[pl.ds(0, boxes)], S.at[pl.ds(0, boxes)], rsem.at[k]).wait()

    def spot(h, drow, piece, which):
        a, b = pos(h)
        return sub(h, c, wrap(b + OFFS[drow]), wrap(a + OFFS[piece]), zof(which))

    def p2_send(h, piece, which, src=None):
        j = spot(h, 0, piece, which)
        for side in (0, 1):
            num = P2 + 4 * piece + 2 * which + side
            if piece < 2:
                send_box(h, num, j, ring(h, 2, side), src)
            else:
                send(h, num, j, ring(h, 2, side), src=src)

    def p2_recv(h, piece, which):
        for side in (0, 1):
            recv(h, P2 + 4 * piece + 2 * which + side, 1 if piece < 2 else 2)

    def f2_send(h, piece, which):
        j = spot(h, 1 if which == 0 else 2, piece, which)
        num = F2 + 2 * piece + which
        if piece < 2:
            send_box(h, num, j, ring(h, 2, which))
        else:
            send(h, num, j, ring(h, 2, which))

    def f2_recv(h, piece):
        for side in (0, 1):
            recv(h, F2 + 2 * piece + side, 1 if piece < 2 else 2)

    def px_send(h, piece, drow, which):
        send_box(h, PX + 6 * piece + 2 * (drow - 1) + which, spot(h, drow, piece, which),
                 partner if piece == 0 else zpart)

    def px_recv(h, piece, drow):
        for which in (0, 1):
            recv(h, PX + 6 * piece + 2 * (drow - 1) + which, 1)

    def encode(j0):
        rows = S[pl.ds(2 * j0, 4)].reshape(256, SZ)
        o = dot_nt(E16[...], rows)
        top, low = o[0:8], o[8:16]
        lane = lax.broadcasted_iota(jnp.int32, (8, 128), 1) % 64
        for half in range(2):
            t = top[:, 128 * half:128 * half + 128]
            u = low[:, 128 * half:128 * half + 128]
            turned = jnp.where(lane < 32, -pltpu.roll(u, 96, 1), pltpu.roll(u, 32, 1))
            W[pl.ds(pl.multiple_of(8 * j0 + 8 * half, 8), 8), :] = t + turned

    def pair(h, c_, drow, piece):
        a, b = pos(h)
        return sub(h, c_, wrap(b + OFFS[drow]), wrap(a + OFFS[piece]), 0)

    earlier = []

    def finish(pairs):
        for h, drow, piece in pairs:
            send(h, SIB + 4 * drow + piece, pair(h, c, drow, piece), sib, n=2)
        for h, drow, piece in pairs:
            encode(pair(h, c, drow, piece))
        for h, drow, piece in earlier:
            recv(h, SIB + 4 * drow + piece, 4)
        for h, drow, piece in earlier:
            encode(pair(h, 1 - c, drow, piece))
        earlier[:] = pairs

    local = []
    for h in (0, 1):
        own = spot(h, 0, 0, 0)
        src = src_ref.at[pl.ds(2 * h, 2)]
        for side in (0, 1):
            send(h, P1 + side, own, ring(h, 1, side), src=src)
        send(h, ZX, own, zpart, src=src)
        cp = pltpu.make_async_copy(src, at(own), lsem.at[h])
        cp.start()
        local.append(cp)
    for h in (0, 1):
        p2_send(h, 0, 0, src=src_ref.at[pl.ds(2 * h + zl, 1)])

    S[pl.ds(256, 2)] = jnp.zeros((2, 64, SZ), BF)
    cell = cell_ref[...]
    cx, cy, cz = cell // 32, cell // 4 % 8, cell % 4
    cell_in = cx * 32 + cz * 8 + cy
    row = lax.broadcasted_iota(jnp.int32, (256, 256), 0)
    col = lax.broadcasted_iota(jnp.int32, (256, 256), 1)
    row1 = lax.broadcasted_iota(jnp.int32, (256, 1), 0)

    def hot(cond):
        return jnp.where(cond, 1.0, 0.0).astype(BF)

    QI[...] = dot_nt(hot(box_of_input(row1) == col), hot(row == cell_in)).astype(BF)
    QO[...] = dot_nt(hot(4 * (row1 % 64) + row1 // 64 == col), hot(row == cell)).astype(BF)

    in_copies[0].wait()
    two_rows = ENC2[...].astype(F32)
    E16[...] = jnp.where(lax.rem(bi, 2) == 1, two_rows[:, 8:16], two_rows[:, 0:8]).reshape(16, SZ).astype(BF)

    in_copies[1].wait()
    d_i = lax.broadcasted_iota(jnp.int32, (256, 128), 0) % 16
    l_i = lax.broadcasted_iota(jnp.int32, (256, 128), 1)
    ly, lz = l_i // 8, l_i % 8
    close = (((d_i <= 1) | (d_i == 15)) & ((ly <= 1) | (ly == 15)) & ((lz <= 1) | (lz == 7)))
    kept = jnp.where(close, 0.0, KER[...].reshape(256, 128))
    k_hi = kept.astype(BF)
    k_lo = (kept - k_hi.astype(F32)).astype(BF)
    lane512 = lax.broadcasted_iota(jnp.int32, (128, 512), 1)
    take = (lane512 % 64) // 4 * 8 + (lane512 % 4 - lane512 // 128 + 8) % 8
    spread = hot(lax.broadcasted_iota(jnp.int32, (128, 512), 0) == take)
    BASE[...] = (jnp.dot(k_hi, spread, preferred_element_type=F32)
                 + jnp.dot(k_lo, spread, preferred_element_type=F32))

    def build_d(mine):
        col = pl.multiple_of(128 * (zl if mine else 1 - zl), 128)
        dr = DEC[0, :, pl.ds(col, 128)].astype(F32).reshape(64, 1, 8, 128)
        di = DEC[1, :, pl.ds(col, 128)].astype(F32).reshape(64, 1, 8, 128)
        left = jnp.concatenate([dr, -di], axis=1).reshape(1024, 128)
        right = jnp.concatenate([di, dr], axis=1).reshape(1024, 128)
        D[0 if mine else 1] = jnp.concatenate([left, right], axis=1).astype(BF)

    lane = lax.broadcasted_iota(jnp.int32, (8, 128), 1)

    def build_t(k):
        for ri in range(2):
            rows = BASE[pl.ds(pl.multiple_of(32 * k + 16 * ri, 16), 16), :]
            one, two = {}, {}
            for dx in range(-7, 8):
                line = rows[dx % 16:dx % 16 + 1, :]
                one[dx] = [pltpu.roll(jnp.broadcast_to(line[:, 128 * s:128 * s + 128], (8, 128)),
                                      0, 1, stride=4, stride_axis=0) for s in range(4)]
            for d in range(-7, 7):
                two[d] = [jnp.where(lane % 64 < 32, one[d][s], pltpu.roll(one[d + 1][s], 32, 1))
                          for s in range(4)]
            four = {d: [jnp.where(lane < 64, two[d][s], two[d + 2][s]) for s in range(4)]
                    for d in range(-7, 5)}
            wide = jnp.concatenate([
                jnp.concatenate([four[-sx][s], four[4 - sx][s]], axis=1)
                for sx in range(8) for s in range(4)], axis=0)
            hi = wide.astype(BF)
            lo = (wide - hi.astype(F32)).astype(BF)
            for part, val in enumerate((hi, lo)):
                first = dot_nt(QO[...], val).astype(BF)
                TT[k, part, ri] = dot_nt(first, QI[...]).astype(BF)

    def step_t(k):
        lax.fori_loop(k, k + 1, lambda n, _: (build_t(n), 0)[1], 0)

    def step_t(k):
        lax.fori_loop(k, k + 1, lambda n, _: (build_t(n), 0)[1], 0)

    for cp in local:
        cp.wait()
    both = (0, 1)

    for h in both:
        for side in both:
            recv(h, P1 + side)
        send(h, F1, spot(h, 0, 1, 0), ring(h, 1, 0))
        p2_send(h, 1, 0)
        p2_send(h, 2, 0)
    for h in both:
        recv(h, ZX)
        for side in both:
            send(h, P1 + 2 + side, spot(h, 0, 0, 1), ring(h, 1, side))
        p2_send(h, 0, 1)
    for h in both:
        p2_recv(h, 0, 0)
        f2_send(h, 0, 0)
        px_send(h, 0, 1, 0)
        px_send(h, 0, 2, 0)
    finish([(h, 0, 0) for h in both])
    step_t(0)
    for h in both:
        for side in both:
            recv(h, P1 + 2 + side)
        send(h, F1 + 1, spot(h, 0, 2, 1), ring(h, 1, 1))
        p2_send(h, 1, 1)
        p2_send(h, 2, 1)
    finish([(h, 0, piece) for piece in (1, 2) for h in both])

    def p2_relay(h, piece, which):
        p2_recv(h, piece, which)
        f2_send(h, piece, which)
        if piece < 2:
            px_send(h, piece, 1, which)
            px_send(h, piece, 2, which)

    def f2_relay(h, piece):
        f2_recv(h, piece)
        px_send(h, piece, 3, 0)
        px_send(h, piece, 3, 1)

    for h in both:
        p2_relay(h, 0, 1)
        p2_relay(h, 1, 0)
    step_t(1)
    for h in both:
        for side in both:
            recv(h, F1 + side)
        p2_send(h, 3, 0)
        p2_send(h, 3, 1)
    finish([(h, 0, 3) for h in both])
    step_t(2)
    for h in both:
        f2_relay(h, 0)
        p2_relay(h, 1, 1)
    step_t(3)
    for h in both:
        p2_relay(h, 2, 0)
        p2_relay(h, 2, 1)
    finish([(h, drow, 2) for drow in (1, 2) for h in both])
    step_t(4)
    for h in both:
        f2_relay(h, 1)
    for h in both:
        for drow in (1, 2):
            px_recv(h, 0, drow)
    finish([(h, drow, 0) for drow in (1, 2) for h in both])
    step_t(5)
    for h in both:
        p2_relay(h, 3, 0)
        p2_relay(h, 3, 1)
    finish([(h, drow, 3) for drow in (1, 2) for h in both])
    step_t(6)
    for h in both:
        for drow in (1, 2):
            px_recv(h, 1, drow)
    finish([(h, drow, 1) for drow in (1, 2) for h in both])
    step_t(7)
    in_copies[2].wait()
    build_d(False)
    build_d(True)
    for h in both:
        px_recv(h, 0, 3)
        f2_recv(h, 2)
    finish([(h, 3, piece) for piece in (0, 2) for h in both])
    for h in both:
        px_recv(h, 1, 3)
    finish([(h, 3, 1) for h in both])
    for h in both:
        f2_recv(h, 3)
    finish([(h, 3, 3) for h in both])
    finish([])

    pl.semaphore_signal(ready, inc=1, device_id=partner, device_id_type=MESH)
    lane64 = lax.broadcasted_iota(jnp.int32, (256, 64), 1)
    quarter = lax.broadcasted_iota(jnp.int32, (64, 128), 1) // 32

    def translate(k, _):
        v = W[pl.ds(k, 128, stride=8), :]
        e = jnp.concatenate([v[:, 0:64], v[:, 64:128]], axis=0)
        hi = e.astype(BF)
        lo = (e - hi.astype(F32)).astype(BF)
        t_hi = TT[k, 0].reshape(512, 256)
        t_lo = TT[k, 1].reshape(512, 256)
        nn = (((1,), (0,)), ((), ()))
        wide = lax.dot_general(t_hi, jnp.concatenate([hi, lo], axis=1), nn, preferred_element_type=F32)
        f = wide[:, 0:64] + wide[:, 64:128]
        f = f + lax.dot_general(t_lo, hi, nn, preferred_element_type=F32)
        fr, fi = f[0:256], f[256:512]
        swapped = jnp.concatenate([fi[:, 32:64], fi[:, 0:32]], axis=1)
        far = fr + jnp.where(lane64 < 32, -swapped, swapped)
        far = jnp.concatenate([far, far], axis=1)
        far_sw = pltpu.roll(far, 32, 1)
        for ri in range(2):
            val = None
            for q in range(4):
                use = far if (q - ri) % 2 == 0 else far_sw
                block = use[64 * q:64 * q + 64]
                val = block if val is None else jnp.where(quarter == q, block, val)
            V[pl.ds(8 * ri + k, 64, stride=16), :] = val
        return 0

    lax.fori_loop(0, KD, translate, 0, unroll=2)
    SEND[...] = V[...].astype(BF).reshape(64, 16, 128)
    R[pl.ds(bi, 1)] = SEND[pl.ds(bi, 1)]

    def scatter(t, _):
        dst = lax.rem(bi + t, NB)
        pltpu.make_async_remote_copy(
            src_ref=SEND.at[dst], dst_ref=R.at[bi], send_sem=a2s.at[0], recv_sem=a2r.at[0],
            device_id=(dst, zl), device_id_type=MESH).start()
        return 0

    pl.semaphore_wait(ready, 1)
    lax.fori_loop(1, NB, scatter, 0)

    def near_box(q, _):
        blocks = NBV[q]
        xs = jnp.concatenate(
            [S[jnp.where(mask_ref[q, s] == 1, slot_of_box(list_ref[q, s]), 256)]
             for s in range(SLOTS)], axis=1)
        bs = jnp.concatenate([blocks[s] for s in range(SLOTS)], axis=1)
        n = dot_nt(xs, bs)
        NEAR[q, 0] = n[0:32, 0:256] - n[32:64, 256:512]
        NEAR[q, 1] = n[32:64, 0:256] + n[0:32, 256:512]
        return 0

    for cp in nb_copies:
        cp.wait()
    lax.fori_loop(0, PER, near_box, 0)

    mine = pl.multiple_of(128 * zl, 128)
    theirs = pl.multiple_of(128 * (1 - zl), 128)
    NS[...] = NEAR[:, :, :, pl.ds(theirs, 128)]
    near_out = pltpu.make_async_remote_copy(
        src_ref=NS, dst_ref=NR, send_sem=pss.at[0], recv_sem=psr.at[0],
        device_id=partner, device_id_type=MESH)
    near_out.start()

    whole = R.at[pl.ds(0, NB - 1)]
    pltpu.make_async_copy(whole, whole, a2r.at[0]).wait()
    got = R[...].reshape(1024, 128)

    def decode(which):
        return lax.dot_general(got, D[which], (((0,), (0,)), ((), ())), preferred_element_type=F32)

    FS[...] = decode(1).astype(BF)
    far_out = pltpu.make_async_remote_copy(
        src_ref=FS, dst_ref=FR, send_sem=pss.at[1], recv_sem=psr.at[1],
        device_id=partner, device_id_type=MESH)
    far_out.start()
    far = decode(0)
    near_out.wait()
    for q in range(4):
        for ro in range(2):
            out_ref[q, ro] = (far[32 * q:32 * q + 32, 128 * ro:128 * ro + 128]
                              + NEAR[q, ro, :, pl.ds(mine, 128)] + NR[q, ro])
    sent = SEND.at[pl.ds(0, NB - 1)]
    pltpu.make_async_copy(sent, sent, a2s.at[0]).wait()
    for cp in started:
        cp.wait_send()
    far_out.wait()
    for q in range(4):
        for ro in range(2):
            out_ref[q, ro] += FR[32 * q:32 * q + 32, 128 * ro:128 * ro + 128].astype(F32)


def on_device(sources, encode, kernel, decode, near_blocks, near_list, near_mask, box_cell):
    smem = pl.BlockSpec(memory_space=pltpu.SMEM)
    hbm = pl.BlockSpec(memory_space=pl.ANY)
    vm = pl.BlockSpec(memory_space=pltpu.VMEM)
    n_sem = 2 * HALF
    return pl.pallas_call(
        body,
        out_shape=jax.ShapeDtypeStruct((PER, 2, RHS, 128), F32),
        in_specs=[smem, smem, vm, hbm, hbm, hbm, hbm, hbm],
        out_specs=vm,
        scratch_shapes=[
            pltpu.VMEM((258, 64, SZ), BF),
            pltpu.VMEM((1024, 128), F32),
            pltpu.VMEM((KD, 2, 2, 256, 256), BF),
            pltpu.VMEM((2, 1024, 256), BF),
            pltpu.VMEM((1024, 128), F32),
            pltpu.VMEM((NB, 16, 128), BF),
            pltpu.VMEM((NB, 16, 128), BF),
            pltpu.VMEM((PER, SLOTS, 512, SZ), BF),
            pltpu.VMEM((PER, 2, RHS, SZ), F32),
            pltpu.VMEM((PER, 2, RHS, 128), F32),
            pltpu.VMEM((PER, 2, RHS, 128), F32),
            pltpu.VMEM((128, 256), BF),
            pltpu.VMEM((128, 256), BF),
            pltpu.VMEM((256, 256), BF),
            pltpu.VMEM((256, 256), BF),
            pltpu.VMEM((256, 512), F32),
            pltpu.VMEM((2, 16, SZ), BF),
            pltpu.VMEM((16, SZ), BF),
            pltpu.VMEM((KD, 2, 16, 128), F32),
            pltpu.VMEM((2, 512, SZ), BF),
            pltpu.SemaphoreType.DMA((n_sem,)),
            pltpu.SemaphoreType.DMA((n_sem,)),
            pltpu.SemaphoreType.DMA((2,)),
            pltpu.SemaphoreType.DMA((PER,)),
            pltpu.SemaphoreType.DMA((3,)),
            pltpu.SemaphoreType.DMA((1,)),
            pltpu.SemaphoreType.DMA((1,)),
            pltpu.SemaphoreType.DMA((2,)),
            pltpu.SemaphoreType.DMA((2,)),
            pltpu.SemaphoreType.REGULAR,
        ],
        compiler_params=pltpu.CompilerParams(
            collective_id=0, has_side_effects=True, vmem_limit_bytes=56 * 2**20),
        name="fmm",
    )(near_list, near_mask, box_cell.reshape(1, 256), sources.reshape(PER, 64, SZ), encode, kernel,
      decode, near_blocks.reshape(PER, SLOTS, 512, SZ))


def solution(mesh):
    in_specs = (
        P("box", None, None, None),
        P(None, "dir", None),
        P(("dir", "box"), None, None, None),
        P(None, "dir", None),
        P("box", "dir", None, None, None),
        P("box", "dir"),
        P("box", "dir"),
        P(),
    )
    return jax.shard_map(
        on_device, mesh=mesh, in_specs=in_specs, out_specs=P("box", None, None, "dir"),
        check_vma=False)
```

```python
import jax
import jax.numpy as jnp
from jax import lax
from jax.experimental import pallas as pl
from jax.experimental.pallas import tpu as pltpu
from jax.sharding import PartitionSpec as P

MESH = pl.DeviceIdType.MESH
BF = jnp.bfloat16
F32 = jnp.float32

NB = 64
PER = 4
KD = 8
RHS = 32
SLOTS = 14
SZ = 256

ZX = 0
P1 = 1
F1 = 5
P2 = 7
F2 = 23
SIB = 31
PX = 47
HALF = 59
OFFS = (0, -1, 1, 2)


def box_of_input(i):
    w, j = i // 128, i % 128
    h, c, p2, p1, z = j // 64, j // 32 % 2, j // 8 % 4, j // 2 % 4, j % 2
    y = jnp.where(h == 0, p2, p1)
    x = jnp.where(h == 0, p1, p2)
    return (((y * 2 + z) * 4 + x) * 2 + c) * 4 + 2 * h + w


def slot_of_box(v):
    w, h, c = lax.rem(v, 2), lax.rem(v // 2, 2), lax.rem(v // 4, 2)
    x, z, y = lax.rem(v // 8, 4), lax.rem(v // 32, 2), v // 64
    first = 8 * y + 2 * x
    second = 8 * x + 2 * y
    return 2 * (h * 64 + c * 32 + jnp.where(h == 1, second, first) + z) + w


def dot_nt(a, b):
    return lax.dot_general(a, b, (((1,), (1,)), ((), ())), preferred_element_type=F32)


def body(list_ref, mask_ref, cell_ref, src_ref, enc_hbm, ker_hbm, dec_hbm, nb_hbm, out_ref,
         S, W, TT, D, V, SEND, R, NBV, NEAR, NS, NR, FS, FR, QI, QO, BASE, ENC2, E16, KER, DEC,
         ssem, rsem, lsem, nsem, isem, a2s, a2r, pss, psr, ready):
    bi = lax.axis_index("box")
    zl = lax.axis_index("dir")
    c = lax.rem(bi, 2)
    x = lax.rem(bi // 2, 4)
    zh = lax.rem(bi // 8, 2)
    y = bi // 16

    def dev(y_, zh_, x_, c_):
        return ((y_ * 2 + zh_) * 4 + x_) * 2 + c_

    def wrap(v):
        return lax.rem(v + 8, 4)

    zpart = (dev(y, 1 - zh, x, c), 1 - zl)
    sib = (dev(y, zh, x, 1 - c), zl)
    partner = (bi, 1 - zl)

    right, left = (dev(y, zh, wrap(x + 1), c), zl), (dev(y, zh, wrap(x - 1), c), zl)
    up, down = (dev(wrap(y + 1), zh, x, c), zl), (dev(wrap(y - 1), zh, x, c), zl)
    bar = pltpu.get_barrier_semaphore()
    for other in (right, left, up, down, zpart, sib, partner):
        pl.semaphore_signal(bar, inc=1, device_id=other, device_id_type=MESH)

    in_copies = [
        pltpu.make_async_copy(enc_hbm.at[:, pl.ds(pl.multiple_of(16 * (bi // 2), 16), 16), :], ENC2, isem.at[0]),
        pltpu.make_async_copy(ker_hbm, KER, isem.at[1]),
        pltpu.make_async_copy(dec_hbm, DEC, isem.at[2])]
    for cp in in_copies:
        cp.start()
    nb_copies = [pltpu.make_async_copy(nb_hbm.at[q], NBV.at[q], nsem.at[q]) for q in range(PER)]
    for cp in nb_copies:
        cp.start()
    pl.semaphore_wait(bar, 7)

    def pos(h):
        return (x, y) if h == 0 else (y, x)

    def ring(h, level, side):
        step = 1 if side == 0 else -1
        along_x = (h == 0) == (level == 1)
        if along_x:
            return (dev(y, zh, wrap(x + step), c), zl)
        return (dev(wrap(y + step), zh, x, c), zl)

    def sub(h, c_, p2, p1, z):
        return h * 64 + c_ * 32 + p2 * 8 + p1 * 2 + z

    def zof(which):
        return zh if which == 0 else 1 - zh

    def at(j, n=1):
        return S.at[pl.ds(2 * j, 2 * n)]

    started = []

    def copy(h, num, src, dst, device):
        cp = pltpu.make_async_remote_copy(
            src_ref=src, dst_ref=dst,
            send_sem=ssem.at[h * HALF + num], recv_sem=rsem.at[h * HALF + num],
            device_id=device, device_id_type=MESH)
        started.append(cp)
        held[h].append(cp)

    held = ([], [])

    def flush():
        a, b = held
        for n in range(max(len(a), len(b))):
            for side in (a, b):
                if n < len(side):
                    side[n].start()
        a.clear()
        b.clear()

    def send(h, num, j, device, n=1, src=None):
        copy(h, num, at(j, n) if src is None else src, at(j, n), device)

    def send_box(h, num, j, device, src=None):
        one = S.at[pl.ds(2 * j + zl, 1)]
        copy(h, num, one if src is None else src, one, device)

    def recv(h, num, boxes=2):
        k = h * HALF + num
        pltpu.make_async_copy(S.at[pl.ds(0, boxes)], S.at[pl.ds(0, boxes)], rsem.at[k]).wait()

    def spot(h, drow, piece, which):
        a, b = pos(h)
        return sub(h, c, wrap(b + OFFS[drow]), wrap(a + OFFS[piece]), zof(which))

    def p2_send(h, piece, which, src=None):
        j = spot(h, 0, piece, which)
        for side in (0, 1):
            num = P2 + 4 * piece + 2 * which + side
            if piece < 2:
                send_box(h, num, j, ring(h, 2, side), src)
            else:
                send(h, num, j, ring(h, 2, side), src=src)

    def p2_recv(h, piece, which):
        for side in (0, 1):
            recv(h, P2 + 4 * piece + 2 * which + side, 1 if piece < 2 else 2)

    def f2_send(h, piece, which):
        j = spot(h, 1 if which == 0 else 2, piece, which)
        num = F2 + 2 * piece + which
        if piece < 2:
            send_box(h, num, j, ring(h, 2, which))
        else:
            send(h, num, j, ring(h, 2, which))

    def f2_recv(h, piece):
        for side in (0, 1):
            recv(h, F2 + 2 * piece + side, 1 if piece < 2 else 2)

    def px_send(h, piece, drow, which):
        send_box(h, PX + 6 * piece + 2 * (drow - 1) + which, spot(h, drow, piece, which),
                 partner if piece == 0 else zpart)

    def px_recv(h, piece, drow):
        for which in (0, 1):
            recv(h, PX + 6 * piece + 2 * (drow - 1) + which, 1)

    def encode(j0):
        rows = S[pl.ds(2 * j0, 4)].reshape(256, SZ)
        o = dot_nt(E16[...], rows)
        top, low = o[0:8], o[8:16]
        lane = lax.broadcasted_iota(jnp.int32, (8, 128), 1) % 64
        for half in range(2):
            t = top[:, 128 * half:128 * half + 128]
            u = low[:, 128 * half:128 * half + 128]
            turned = jnp.where(lane < 32, -pltpu.roll(u, 96, 1), pltpu.roll(u, 32, 1))
            W[pl.ds(pl.multiple_of(8 * j0 + 8 * half, 8), 8), :] = t + turned

    def pair(h, c_, drow, piece):
        a, b = pos(h)
        return sub(h, c_, wrap(b + OFFS[drow]), wrap(a + OFFS[piece]), 0)

    earlier = []

    def finish(pairs):
        flush()
        for h, drow, piece in pairs:
            send(h, SIB + 4 * drow + piece, pair(h, c, drow, piece), sib, n=2)
        flush()
        for h, drow, piece in pairs:
            encode(pair(h, c, drow, piece))
        for h, drow, piece in earlier:
            recv(h, SIB + 4 * drow + piece, 4)
        for h, drow, piece in earlier:
            encode(pair(h, 1 - c, drow, piece))
        earlier[:] = pairs

    local = []
    for h in (0, 1):
        own = spot(h, 0, 0, 0)
        src = src_ref.at[pl.ds(2 * h, 2)]
        for side in (0, 1):
            send(h, P1 + side, own, ring(h, 1, side), src=src)
        send(h, ZX, own, zpart, src=src)
        cp = pltpu.make_async_copy(src, at(own), lsem.at[h])
        cp.start()
        local.append(cp)
    for h in (0, 1):
        p2_send(h, 0, 0, src=src_ref.at[pl.ds(2 * h + zl, 1)])
    flush()

    S[pl.ds(256, 2)] = jnp.zeros((2, 64, SZ), BF)
    cell = cell_ref[...]
    cx, cy, cz = cell // 32, cell // 4 % 8, cell % 4
    cell_in = cx * 32 + cz * 8 + cy
    row = lax.broadcasted_iota(jnp.int32, (256, 256), 0)
    col = lax.broadcasted_iota(jnp.int32, (256, 256), 1)
    row1 = lax.broadcasted_iota(jnp.int32, (256, 1), 0)

    def hot(cond):
        return jnp.where(cond, 1.0, 0.0).astype(BF)

    QI[...] = dot_nt(hot(box_of_input(row1) == col), hot(row == cell_in)).astype(BF)
    QO[...] = dot_nt(hot(4 * (row1 % 64) + row1 // 64 == col), hot(row == cell)).astype(BF)

    in_copies[0].wait()
    two_rows = ENC2[...].astype(F32)
    E16[...] = jnp.where(lax.rem(bi, 2) == 1, two_rows[:, 8:16], two_rows[:, 0:8]).reshape(16, SZ).astype(BF)

    in_copies[1].wait()
    d_i = lax.broadcasted_iota(jnp.int32, (256, 128), 0) % 16
    l_i = lax.broadcasted_iota(jnp.int32, (256, 128), 1)
    ly, lz = l_i // 8, l_i % 8
    close = (((d_i <= 1) | (d_i == 15)) & ((ly <= 1) | (ly == 15)) & ((lz <= 1) | (lz == 7)))
    kept = jnp.where(close, 0.0, KER[...].reshape(256, 128))
    k_hi = kept.astype(BF)
    k_lo = (kept - k_hi.astype(F32)).astype(BF)
    lane512 = lax.broadcasted_iota(jnp.int32, (128, 512), 1)
    take = (lane512 % 64) // 4 * 8 + (lane512 % 4 - lane512 // 128 + 8) % 8
    spread = hot(lax.broadcasted_iota(jnp.int32, (128, 512), 0) == take)
    BASE[...] = (jnp.dot(k_hi, spread, preferred_element_type=F32)
                 + jnp.dot(k_lo, spread, preferred_element_type=F32))

    def build_d(mine):
        col = pl.multiple_of(128 * (zl if mine else 1 - zl), 128)
        dr = DEC[0, :, pl.ds(col, 128)].astype(F32).reshape(64, 1, 8, 128)
        di = DEC[1, :, pl.ds(col, 128)].astype(F32).reshape(64, 1, 8, 128)
        left = jnp.concatenate([dr, -di], axis=1).reshape(1024, 128)
        right = jnp.concatenate([di, dr], axis=1).reshape(1024, 128)
        D[0 if mine else 1] = jnp.concatenate([left, right], axis=1).astype(BF)

    lane = lax.broadcasted_iota(jnp.int32, (8, 128), 1)

    def build_t(k):
        for ri in range(2):
            rows = BASE[pl.ds(pl.multiple_of(32 * k + 16 * ri, 16), 16), :]
            one, two = {}, {}
            for dx in range(-7, 8):
                line = rows[dx % 16:dx % 16 + 1, :]
                one[dx] = [pltpu.roll(jnp.broadcast_to(line[:, 128 * s:128 * s + 128], (8, 128)),
                                      0, 1, stride=4, stride_axis=0) for s in range(4)]
            for d in range(-7, 7):
                two[d] = [jnp.where(lane % 64 < 32, one[d][s], pltpu.roll(one[d + 1][s], 32, 1))
                          for s in range(4)]
            four = {d: [jnp.where(lane < 64, two[d][s], two[d + 2][s]) for s in range(4)]
                    for d in range(-7, 5)}
            wide = jnp.concatenate([
                jnp.concatenate([four[-sx][s], four[4 - sx][s]], axis=1)
                for sx in range(8) for s in range(4)], axis=0)
            hi = wide.astype(BF)
            lo = (wide - hi.astype(F32)).astype(BF)
            for part, val in enumerate((hi, lo)):
                first = dot_nt(QO[...], val).astype(BF)
                TT[k, part, ri] = dot_nt(first, QI[...]).astype(BF)

    def step_t(k):
        flush()
        lax.fori_loop(k, k + 1, lambda n, _: (build_t(n), 0)[1], 0)

    def step_t(k):
        flush()
        lax.fori_loop(k, k + 1, lambda n, _: (build_t(n), 0)[1], 0)

    for cp in local:
        cp.wait()
    both = (0, 1)

    def p2_relay(h, piece, which):
        p2_recv(h, piece, which)
        if piece < 2:
            px_send(h, piece, 1, which)
            px_send(h, piece, 2, which)
        f2_send(h, piece, which)

    def f2_relay(h, piece):
        f2_recv(h, piece)
        px_send(h, piece, 3, 0)
        px_send(h, piece, 3, 1)

    def relay(*steps):
        for piece, which in steps:
            for h in both:
                p2_relay(h, piece, which)
            flush()

    for h in both:
        for side in both:
            recv(h, P1 + side)
        send(h, F1, spot(h, 0, 1, 0), ring(h, 1, 0))
    flush()
    for h in both:
        recv(h, ZX)
        for side in both:
            send(h, P1 + 2 + side, spot(h, 0, 0, 1), ring(h, 1, side))
    flush()
    for h in both:
        p2_send(h, 1, 0)
        p2_send(h, 0, 1)
        p2_send(h, 2, 0)
    flush()
    relay((0, 0))
    finish([(h, 0, 0) for h in both])
    step_t(0)
    for h in both:
        for side in both:
            recv(h, P1 + 2 + side)
        send(h, F1 + 1, spot(h, 0, 2, 1), ring(h, 1, 1))
    flush()
    for h in both:
        recv(h, F1)
        p2_send(h, 3, 0)
    flush()
    for h in both:
        p2_send(h, 1, 1)
        p2_send(h, 2, 1)
    finish([(h, 0, piece) for piece in (1, 2) for h in both])
    relay((0, 1), (1, 0))
    step_t(1)
    for h in both:
        recv(h, F1 + 1)
        p2_send(h, 3, 1)
    finish([(h, 0, 3) for h in both])
    step_t(2)
    for h in both:
        f2_relay(h, 0)
    flush()
    relay((2, 0), (1, 1))
    step_t(3)
    relay((3, 0), (2, 1))
    finish([(h, drow, 2) for drow in (1, 2) for h in both])
    step_t(4)
    for h in both:
        f2_relay(h, 1)
    flush()
    relay((3, 1))
    finish([(h, drow, 3) for drow in (1, 2) for h in both])
    for h in both:
        for drow in (1, 2):
            px_recv(h, 0, drow)
    finish([(h, drow, 0) for drow in (1, 2) for h in both])
    step_t(5)
    for h in both:
        for drow in (1, 2):
            px_recv(h, 1, drow)
    finish([(h, drow, 1) for drow in (1, 2) for h in both])
    step_t(6)
    step_t(7)
    in_copies[2].wait()
    build_d(False)
    build_d(True)
    for h in both:
        px_recv(h, 0, 3)
        f2_recv(h, 2)
    finish([(h, 3, piece) for piece in (0, 2) for h in both])
    for h in both:
        px_recv(h, 1, 3)
    finish([(h, 3, 1) for h in both])
    for h in both:
        f2_recv(h, 3)
    finish([(h, 3, 3) for h in both])
    finish([])

    pl.semaphore_signal(ready, inc=1, device_id=partner, device_id_type=MESH)
    lane64 = lax.broadcasted_iota(jnp.int32, (256, 64), 1)
    quarter = lax.broadcasted_iota(jnp.int32, (64, 128), 1) // 32

    def translate(k, _):
        v = W[pl.ds(k, 128, stride=8), :]
        e = jnp.concatenate([v[:, 0:64], v[:, 64:128]], axis=0)
        hi = e.astype(BF)
        lo = (e - hi.astype(F32)).astype(BF)
        t_hi = TT[k, 0].reshape(512, 256)
        t_lo = TT[k, 1].reshape(512, 256)
        nn = (((1,), (0,)), ((), ()))
        wide = lax.dot_general(t_hi, jnp.concatenate([hi, lo], axis=1), nn, preferred_element_type=F32)
        f = wide[:, 0:64] + wide[:, 64:128]
        f = f + lax.dot_general(t_lo, hi, nn, preferred_element_type=F32)
        fr, fi = f[0:256], f[256:512]
        swapped = jnp.concatenate([fi[:, 32:64], fi[:, 0:32]], axis=1)
        far = fr + jnp.where(lane64 < 32, -swapped, swapped)
        far = jnp.concatenate([far, far], axis=1)
        far_sw = pltpu.roll(far, 32, 1)
        for ri in range(2):
            val = None
            for q in range(4):
                use = far if (q - ri) % 2 == 0 else far_sw
                block = use[64 * q:64 * q + 64]
                val = block if val is None else jnp.where(quarter == q, block, val)
            V[pl.ds(8 * ri + k, 64, stride=16), :] = val
        return 0

    lax.fori_loop(0, KD, translate, 0, unroll=4)
    SEND[...] = V[...].astype(BF).reshape(64, 16, 128)
    R[pl.ds(bi, 1)] = SEND[pl.ds(bi, 1)]

    def scatter(t, _):
        dst = lax.rem(bi + t, NB)
        pltpu.make_async_remote_copy(
            src_ref=SEND.at[dst], dst_ref=R.at[bi], send_sem=a2s.at[0], recv_sem=a2r.at[0],
            device_id=(dst, zl), device_id_type=MESH).start()
        return 0

    pl.semaphore_wait(ready, 1)
    lax.fori_loop(1, NB, scatter, 0)

    def near_box(q, _):
        blocks = NBV[q]
        xs = jnp.concatenate(
            [S[jnp.where(mask_ref[q, s] == 1, slot_of_box(list_ref[q, s]), 256)]
             for s in range(SLOTS)], axis=1)
        bs = jnp.concatenate([blocks[s] for s in range(SLOTS)], axis=1)
        n = dot_nt(xs, bs)
        NEAR[q, 0] = n[0:32, 0:256] - n[32:64, 256:512]
        NEAR[q, 1] = n[32:64, 0:256] + n[0:32, 256:512]
        return 0

    for cp in nb_copies:
        cp.wait()
    lax.fori_loop(0, PER, near_box, 0)

    mine = pl.multiple_of(128 * zl, 128)
    theirs = pl.multiple_of(128 * (1 - zl), 128)
    NS[...] = NEAR[:, :, :, pl.ds(theirs, 128)]
    near_out = pltpu.make_async_remote_copy(
        src_ref=NS, dst_ref=NR, send_sem=pss.at[0], recv_sem=psr.at[0],
        device_id=partner, device_id_type=MESH)
    near_out.start()

    whole = R.at[pl.ds(0, NB - 1)]
    pltpu.make_async_copy(whole, whole, a2r.at[0]).wait()
    got = R[...].reshape(1024, 128)

    def decode(which):
        return lax.dot_general(got, D[which], (((0,), (0,)), ((), ())), preferred_element_type=F32)

    FS[...] = decode(1).astype(BF)
    far_out = pltpu.make_async_remote_copy(
        src_ref=FS, dst_ref=FR, send_sem=pss.at[1], recv_sem=psr.at[1],
        device_id=partner, device_id_type=MESH)
    far_out.start()
    far = decode(0)
    near_out.wait()
    for q in range(4):
        for ro in range(2):
            out_ref[q, ro] = (far[32 * q:32 * q + 32, 128 * ro:128 * ro + 128]
                              + NEAR[q, ro, :, pl.ds(mine, 128)] + NR[q, ro])
    sent = SEND.at[pl.ds(0, NB - 1)]
    pltpu.make_async_copy(sent, sent, a2s.at[0]).wait()
    for cp in started:
        cp.wait_send()
    far_out.wait()
    for q in range(4):
        for ro in range(2):
            out_ref[q, ro] += FR[32 * q:32 * q + 32, 128 * ro:128 * ro + 128].astype(F32)


def on_device(sources, encode, kernel, decode, near_blocks, near_list, near_mask, box_cell):
    smem = pl.BlockSpec(memory_space=pltpu.SMEM)
    hbm = pl.BlockSpec(memory_space=pl.ANY)
    vm = pl.BlockSpec(memory_space=pltpu.VMEM)
    n_sem = 2 * HALF
    return pl.pallas_call(
        body,
        out_shape=jax.ShapeDtypeStruct((PER, 2, RHS, 128), F32),
        in_specs=[smem, smem, vm, hbm, hbm, hbm, hbm, hbm],
        out_specs=vm,
        scratch_shapes=[
            pltpu.VMEM((258, 64, SZ), BF),
            pltpu.VMEM((1024, 128), F32),
            pltpu.VMEM((KD, 2, 2, 256, 256), BF),
            pltpu.VMEM((2, 1024, 256), BF),
            pltpu.VMEM((1024, 128), F32),
            pltpu.VMEM((NB, 16, 128), BF),
            pltpu.VMEM((NB, 16, 128), BF),
            pltpu.VMEM((PER, SLOTS, 512, SZ), BF),
            pltpu.VMEM((PER, 2, RHS, SZ), F32),
            pltpu.VMEM((PER, 2, RHS, 128), F32),
            pltpu.VMEM((PER, 2, RHS, 128), F32),
            pltpu.VMEM((128, 256), BF),
            pltpu.VMEM((128, 256), BF),
            pltpu.VMEM((256, 256), BF),
            pltpu.VMEM((256, 256), BF),
            pltpu.VMEM((256, 512), F32),
            pltpu.VMEM((2, 16, SZ), BF),
            pltpu.VMEM((16, SZ), BF),
            pltpu.VMEM((KD, 2, 16, 128), F32),
            pltpu.VMEM((2, 512, SZ), BF),
            pltpu.SemaphoreType.DMA((n_sem,)),
            pltpu.SemaphoreType.DMA((n_sem,)),
            pltpu.SemaphoreType.DMA((2,)),
            pltpu.SemaphoreType.DMA((PER,)),
            pltpu.SemaphoreType.DMA((3,)),
            pltpu.SemaphoreType.DMA((1,)),
            pltpu.SemaphoreType.DMA((1,)),
            pltpu.SemaphoreType.DMA((2,)),
            pltpu.SemaphoreType.DMA((2,)),
            pltpu.SemaphoreType.REGULAR,
        ],
        compiler_params=pltpu.CompilerParams(
            collective_id=0, has_side_effects=True, vmem_limit_bytes=56 * 2**20),
        name="fmm",
    )(near_list, near_mask, box_cell.reshape(1, 256), sources.reshape(PER, 64, SZ), encode, kernel,
      decode, near_blocks.reshape(PER, SLOTS, 512, SZ))


def solution(mesh):
    in_specs = (
        P("box", None, None, None),
        P(None, "dir", None),
        P(("dir", "box"), None, None, None),
        P(None, "dir", None),
        P("box", "dir", None, None, None),
        P("box", "dir"),
        P("box", "dir"),
        P(),
    )
    return jax.shard_map(
        on_device, mesh=mesh, in_specs=in_specs, out_specs=P("box", None, None, "dir"),
        check_vma=False)
```

```python
import jax
import jax.numpy as jnp
from jax import lax
from jax.experimental import pallas as pl
from jax.experimental.pallas import tpu as pltpu
from jax.sharding import PartitionSpec as P

MESH = pl.DeviceIdType.MESH
BF = jnp.bfloat16
F32 = jnp.float32

NB = 64
PER = 4
KD = 8
RHS = 32
SLOTS = 14
SZ = 256

ZX = 0
P1 = 1
F1 = 5
P2 = 7
F2 = 23
SIB = 31
PX = 47
HALF = 59
OFFS = (0, -1, 1, 2)


def box_of_input(i):
    w, j = i // 128, i % 128
    h, c, p2, p1, z = j // 64, j // 32 % 2, j // 8 % 4, j // 2 % 4, j % 2
    y = jnp.where(h == 0, p2, p1)
    x = jnp.where(h == 0, p1, p2)
    return (((y * 2 + z) * 4 + x) * 2 + c) * 4 + 2 * h + w


def slot_of_box(v):
    w, h, c = lax.rem(v, 2), lax.rem(v // 2, 2), lax.rem(v // 4, 2)
    x, z, y = lax.rem(v // 8, 4), lax.rem(v // 32, 2), v // 64
    first = 8 * y + 2 * x
    second = 8 * x + 2 * y
    return 2 * (h * 64 + c * 32 + jnp.where(h == 1, second, first) + z) + w


def dot_nt(a, b):
    return lax.dot_general(a, b, (((1,), (1,)), ((), ())), preferred_element_type=F32)


def body(list_ref, mask_ref, cell_ref, src_ref, enc_hbm, ker_hbm, dec_hbm, nb_hbm, out_ref,
         S, W, TT, D, V, SEND, R, NBV, NEAR, NS, NR, FS, FR, QI, QO, BASE, ENC2, E16, KER, DEC,
         ssem, rsem, lsem, nsem, isem, a2s, a2r, pss, psr, ready):
    bi = lax.axis_index("box")
    zl = lax.axis_index("dir")
    c = lax.rem(bi, 2)
    x = lax.rem(bi // 2, 4)
    zh = lax.rem(bi // 8, 2)
    y = bi // 16

    def dev(y_, zh_, x_, c_):
        return ((y_ * 2 + zh_) * 4 + x_) * 2 + c_

    def wrap(v):
        return lax.rem(v + 8, 4)

    zpart = (dev(y, 1 - zh, x, c), 1 - zl)
    sib = (dev(y, zh, x, 1 - c), zl)
    partner = (bi, 1 - zl)

    right, left = (dev(y, zh, wrap(x + 1), c), zl), (dev(y, zh, wrap(x - 1), c), zl)
    up, down = (dev(wrap(y + 1), zh, x, c), zl), (dev(wrap(y - 1), zh, x, c), zl)
    bar = pltpu.get_barrier_semaphore()
    for other in (right, left, up, down, zpart, sib, partner):
        pl.semaphore_signal(bar, inc=1, device_id=other, device_id_type=MESH)

    in_copies = [
        pltpu.make_async_copy(enc_hbm.at[:, pl.ds(pl.multiple_of(16 * (bi // 2), 16), 16), :], ENC2, isem.at[0]),
        pltpu.make_async_copy(ker_hbm, KER, isem.at[1]),
        pltpu.make_async_copy(dec_hbm, DEC, isem.at[2])]
    for cp in in_copies:
        cp.start()
    nb_copies = [pltpu.make_async_copy(nb_hbm.at[q], NBV.at[q], nsem.at[q]) for q in range(PER)]
    for cp in nb_copies:
        cp.start()
    pl.semaphore_wait(bar, 7)

    def pos(h):
        return (x, y) if h == 0 else (y, x)

    def ring(h, level, side):
        step = 1 if side == 0 else -1
        along_x = (h == 0) == (level == 1)
        if along_x:
            return (dev(y, zh, wrap(x + step), c), zl)
        return (dev(wrap(y + step), zh, x, c), zl)

    def sub(h, c_, p2, p1, z):
        return h * 64 + c_ * 32 + p2 * 8 + p1 * 2 + z

    def zof(which):
        return zh if which == 0 else 1 - zh

    def at(j, n=1):
        return S.at[pl.ds(2 * j, 2 * n)]

    started = []

    def copy(h, num, src, dst, device):
        cp = pltpu.make_async_remote_copy(
            src_ref=src, dst_ref=dst,
            send_sem=ssem.at[h * HALF + num], recv_sem=rsem.at[h * HALF + num],
            device_id=device, device_id_type=MESH)
        started.append(cp)
        held[h].append(cp)

    held = ([], [])

    def flush():
        a, b = held
        for n in range(max(len(a), len(b))):
            for side in (a, b):
                if n < len(side):
                    side[n].start()
        a.clear()
        b.clear()

    def send(h, num, j, device, n=1, src=None):
        copy(h, num, at(j, n) if src is None else src, at(j, n), device)

    def send_box(h, num, j, device, src=None):
        one = S.at[pl.ds(2 * j + zl, 1)]
        copy(h, num, one if src is None else src, one, device)

    def recv(h, num, boxes=2):
        k = h * HALF + num
        pltpu.make_async_copy(S.at[pl.ds(0, boxes)], S.at[pl.ds(0, boxes)], rsem.at[k]).wait()

    def spot(h, drow, piece, which):
        a, b = pos(h)
        return sub(h, c, wrap(b + OFFS[drow]), wrap(a + OFFS[piece]), zof(which))

    def p2_send(h, piece, which, src=None):
        j = spot(h, 0, piece, which)
        for side in (0, 1):
            num = P2 + 4 * piece + 2 * which + side
            if piece < 2:
                send_box(h, num, j, ring(h, 2, side), src)
            else:
                send(h, num, j, ring(h, 2, side), src=src)

    def p2_recv(h, piece, which):
        for side in (0, 1):
            recv(h, P2 + 4 * piece + 2 * which + side, 1 if piece < 2 else 2)

    def f2_send(h, piece, which):
        j = spot(h, 1 if which == 0 else 2, piece, which)
        num = F2 + 2 * piece + which
        if piece < 2:
            send_box(h, num, j, ring(h, 2, which))
        else:
            send(h, num, j, ring(h, 2, which))

    def f2_recv(h, piece):
        for side in (0, 1):
            recv(h, F2 + 2 * piece + side, 1 if piece < 2 else 2)

    def px_send(h, piece, drow, which):
        send_box(h, PX + 6 * piece + 2 * (drow - 1) + which, spot(h, drow, piece, which),
                 partner if piece == 0 else zpart)

    def px_recv(h, piece, drow):
        for which in (0, 1):
            recv(h, PX + 6 * piece + 2 * (drow - 1) + which, 1)

    def encode(j0):
        rows = S[pl.ds(2 * j0, 4)].reshape(256, SZ)
        o = dot_nt(E16[...], rows)
        top, low = o[0:8], o[8:16]
        lane = lax.broadcasted_iota(jnp.int32, (8, 128), 1) % 64
        for half in range(2):
            t = top[:, 128 * half:128 * half + 128]
            u = low[:, 128 * half:128 * half + 128]
            turned = jnp.where(lane < 32, -pltpu.roll(u, 96, 1), pltpu.roll(u, 32, 1))
            W[pl.ds(pl.multiple_of(8 * j0 + 8 * half, 8), 8), :] = t + turned

    def pair(h, c_, drow, piece):
        a, b = pos(h)
        return sub(h, c_, wrap(b + OFFS[drow]), wrap(a + OFFS[piece]), 0)

    earlier = []

    def finish(pairs):
        flush()
        for h, drow, piece in pairs:
            send(h, SIB + 4 * drow + piece, pair(h, c, drow, piece), sib, n=2)
        flush()
        for h, drow, piece in pairs:
            encode(pair(h, c, drow, piece))
        for h, drow, piece in earlier:
            recv(h, SIB + 4 * drow + piece, 4)
        for h, drow, piece in earlier:
            encode(pair(h, 1 - c, drow, piece))
        earlier[:] = pairs

    local = []
    for h in (0, 1):
        own = spot(h, 0, 0, 0)
        src = src_ref.at[pl.ds(2 * h, 2)]
        for side in (0, 1):
            send(h, P1 + side, own, ring(h, 1, side), src=src)
        send(h, ZX, own, zpart, src=src)
        cp = pltpu.make_async_copy(src, at(own), lsem.at[h])
        cp.start()
        local.append(cp)
    for h in (0, 1):
        p2_send(h, 0, 0, src=src_ref.at[pl.ds(2 * h + zl, 1)])
    flush()

    S[pl.ds(256, 2)] = jnp.zeros((2, 64, SZ), BF)
    cell = cell_ref[...]
    cx, cy, cz = cell // 32, cell // 4 % 8, cell % 4
    cell_in = cx * 32 + cz * 8 + cy
    row = lax.broadcasted_iota(jnp.int32, (256, 256), 0)
    col = lax.broadcasted_iota(jnp.int32, (256, 256), 1)
    row1 = lax.broadcasted_iota(jnp.int32, (256, 1), 0)

    def hot(cond):
        return jnp.where(cond, 1.0, 0.0).astype(BF)

    QI[...] = dot_nt(hot(box_of_input(row1) == col), hot(row == cell_in)).astype(BF)
    QO[...] = dot_nt(hot(4 * (row1 % 64) + row1 // 64 == col), hot(row == cell)).astype(BF)

    in_copies[0].wait()
    two_rows = ENC2[...].astype(F32)
    E16[...] = jnp.where(lax.rem(bi, 2) == 1, two_rows[:, 8:16], two_rows[:, 0:8]).reshape(16, SZ).astype(BF)

    in_copies[1].wait()
    d_i = lax.broadcasted_iota(jnp.int32, (256, 128), 0) % 16
    l_i = lax.broadcasted_iota(jnp.int32, (256, 128), 1)
    ly, lz = l_i // 8, l_i % 8
    close = (((d_i <= 1) | (d_i == 15)) & ((ly <= 1) | (ly == 15)) & ((lz <= 1) | (lz == 7)))
    kept = jnp.where(close, 0.0, KER[...].reshape(256, 128))
    k_hi = kept.astype(BF)
    k_lo = (kept - k_hi.astype(F32)).astype(BF)
    lane512 = lax.broadcasted_iota(jnp.int32, (128, 512), 1)
    take = (lane512 % 64) // 4 * 8 + (lane512 % 4 - lane512 // 128 + 8) % 8
    spread = hot(lax.broadcasted_iota(jnp.int32, (128, 512), 0) == take)
    BASE[...] = (jnp.dot(k_hi, spread, preferred_element_type=F32)
                 + jnp.dot(k_lo, spread, preferred_element_type=F32))

    def build_d(mine):
        col = pl.multiple_of(128 * (zl if mine else 1 - zl), 128)
        dr = DEC[0, :, pl.ds(col, 128)].astype(F32).reshape(64, 1, 8, 128)
        di = DEC[1, :, pl.ds(col, 128)].astype(F32).reshape(64, 1, 8, 128)
        left = jnp.concatenate([dr, -di], axis=1).reshape(1024, 128)
        right = jnp.concatenate([di, dr], axis=1).reshape(1024, 128)
        D[0 if mine else 1] = jnp.concatenate([left, right], axis=1).astype(BF)

    lane = lax.broadcasted_iota(jnp.int32, (8, 128), 1)

    def build_t(k):
        for ri in range(2):
            rows = BASE[pl.ds(pl.multiple_of(32 * k + 16 * ri, 16), 16), :]
            one, two = {}, {}
            for dx in range(-7, 8):
                line = rows[dx % 16:dx % 16 + 1, :]
                one[dx] = [pltpu.roll(jnp.broadcast_to(line[:, 128 * s:128 * s + 128], (8, 128)),
                                      0, 1, stride=4, stride_axis=0) for s in range(4)]
            for d in range(-7, 7):
                two[d] = [jnp.where(lane % 64 < 32, one[d][s], pltpu.roll(one[d + 1][s], 32, 1))
                          for s in range(4)]
            four = {d: [jnp.where(lane < 64, two[d][s], two[d + 2][s]) for s in range(4)]
                    for d in range(-7, 5)}
            wide = jnp.concatenate([
                jnp.concatenate([four[-sx][s], four[4 - sx][s]], axis=1)
                for sx in range(8) for s in range(4)], axis=0)
            hi = wide.astype(BF)
            lo = (wide - hi.astype(F32)).astype(BF)
            for part, val in enumerate((hi, lo)):
                first = dot_nt(QO[...], val).astype(BF)
                TT[k, part, ri] = dot_nt(first, QI[...]).astype(BF)

    def step_t(k):
        flush()
        lax.fori_loop(k, k + 1, lambda n, _: (build_t(n), 0)[1], 0)

    def step_t(k):
        flush()
        lax.fori_loop(k, k + 1, lambda n, _: (build_t(n), 0)[1], 0)

    for cp in local:
        cp.wait()
    both = (0, 1)

    def p2_relay(h, piece, which):
        p2_recv(h, piece, which)
        if piece < 2:
            px_send(h, piece, 1, which)
            px_send(h, piece, 2, which)
        f2_send(h, piece, which)

    def f2_relay(h, piece):
        f2_recv(h, piece)
        px_send(h, piece, 3, 0)
        px_send(h, piece, 3, 1)

    def relay(*steps):
        for piece, which in steps:
            for h in both:
                p2_relay(h, piece, which)
            flush()

    for h in both:
        for side in both:
            recv(h, P1 + side)
        send(h, F1, spot(h, 0, 1, 0), ring(h, 1, 0))
    flush()
    for h in both:
        recv(h, ZX)
        for side in both:
            send(h, P1 + 2 + side, spot(h, 0, 0, 1), ring(h, 1, side))
    flush()
    for h in both:
        p2_send(h, 1, 0)
        p2_send(h, 0, 1)
        p2_send(h, 2, 0)
    flush()
    relay((0, 0))
    finish([(h, 0, 0) for h in both])
    step_t(0)
    step_t(1)
    for h in both:
        for side in both:
            recv(h, P1 + 2 + side)
        send(h, F1 + 1, spot(h, 0, 2, 1), ring(h, 1, 1))
    flush()
    for h in both:
        recv(h, F1)
        p2_send(h, 3, 0)
    flush()
    for h in both:
        p2_send(h, 1, 1)
        p2_send(h, 2, 1)
    finish([(h, 0, piece) for piece in (1, 2) for h in both])
    relay((0, 1), (1, 0))
    step_t(2)
    step_t(3)
    for h in both:
        recv(h, F1 + 1)
        p2_send(h, 3, 1)
    finish([(h, 0, 3) for h in both])
    step_t(4)
    step_t(5)
    in_copies[2].wait()
    build_d(False)
    build_d(True)
    for h in both:
        f2_relay(h, 0)
    flush()
    relay((2, 0), (1, 1))
    step_t(6)
    relay((3, 0), (2, 1))
    finish([(h, drow, 2) for drow in (1, 2) for h in both])
    step_t(7)
    for h in both:
        f2_relay(h, 1)
    flush()
    relay((3, 1))
    finish([(h, drow, 3) for drow in (1, 2) for h in both])
    for h in both:
        for drow in (1, 2):
            px_recv(h, 0, drow)
    finish([(h, drow, 0) for drow in (1, 2) for h in both])
    flush()
    for h in both:
        for drow in (1, 2):
            px_recv(h, 1, drow)
    finish([(h, drow, 1) for drow in (1, 2) for h in both])
    flush()
    flush()
    for h in both:
        px_recv(h, 0, 3)
        f2_recv(h, 2)
    finish([(h, 3, piece) for piece in (0, 2) for h in both])
    for h in both:
        px_recv(h, 1, 3)
    finish([(h, 3, 1) for h in both])
    for h in both:
        f2_recv(h, 3)
    finish([(h, 3, 3) for h in both])
    finish([])

    pl.semaphore_signal(ready, inc=1, device_id=partner, device_id_type=MESH)
    lane64 = lax.broadcasted_iota(jnp.int32, (256, 64), 1)
    quarter = lax.broadcasted_iota(jnp.int32, (64, 128), 1) // 32

    def translate(k, _):
        v = W[pl.ds(k, 128, stride=8), :]
        e = jnp.concatenate([v[:, 0:64], v[:, 64:128]], axis=0)
        hi = e.astype(BF)
        lo = (e - hi.astype(F32)).astype(BF)
        t_hi = TT[k, 0].reshape(512, 256)
        t_lo = TT[k, 1].reshape(512, 256)
        nn = (((1,), (0,)), ((), ()))
        wide = lax.dot_general(t_hi, jnp.concatenate([hi, lo], axis=1), nn, preferred_element_type=F32)
        f = wide[:, 0:64] + wide[:, 64:128]
        f = f + lax.dot_general(t_lo, hi, nn, preferred_element_type=F32)
        fr, fi = f[0:256], f[256:512]
        swapped = jnp.concatenate([fi[:, 32:64], fi[:, 0:32]], axis=1)
        far = fr + jnp.where(lane64 < 32, -swapped, swapped)
        far = jnp.concatenate([far, far], axis=1)
        far_sw = pltpu.roll(far, 32, 1)
        for ri in range(2):
            val = None
            for q in range(4):
                use = far if (q - ri) % 2 == 0 else far_sw
                block = use[64 * q:64 * q + 64]
                val = block if val is None else jnp.where(quarter == q, block, val)
            V[pl.ds(8 * ri + k, 64, stride=16), :] = val
        return 0

    lax.fori_loop(0, KD, translate, 0, unroll=4)
    SEND[...] = V[...].astype(BF).reshape(64, 16, 128)
    R[pl.ds(bi, 1)] = SEND[pl.ds(bi, 1)]

    def scatter(t, _):
        dst = lax.rem(bi + t, NB)
        pltpu.make_async_remote_copy(
            src_ref=SEND.at[dst], dst_ref=R.at[bi], send_sem=a2s.at[0], recv_sem=a2r.at[0],
            device_id=(dst, zl), device_id_type=MESH).start()
        return 0

    pl.semaphore_wait(ready, 1)
    lax.fori_loop(1, NB, scatter, 0)

    def near_box(q, _):
        blocks = NBV[q]
        xs = jnp.concatenate(
            [S[jnp.where(mask_ref[q, s] == 1, slot_of_box(list_ref[q, s]), 256)]
             for s in range(SLOTS)], axis=1)
        bs = jnp.concatenate([blocks[s] for s in range(SLOTS)], axis=1)
        n = dot_nt(xs, bs)
        NEAR[q, 0] = n[0:32, 0:256] - n[32:64, 256:512]
        NEAR[q, 1] = n[32:64, 0:256] + n[0:32, 256:512]
        return 0

    for cp in nb_copies:
        cp.wait()
    lax.fori_loop(0, PER, near_box, 0)

    mine = pl.multiple_of(128 * zl, 128)
    theirs = pl.multiple_of(128 * (1 - zl), 128)
    NS[...] = NEAR[:, :, :, pl.ds(theirs, 128)]
    near_out = pltpu.make_async_remote_copy(
        src_ref=NS, dst_ref=NR, send_sem=pss.at[0], recv_sem=psr.at[0],
        device_id=partner, device_id_type=MESH)
    near_out.start()

    whole = R.at[pl.ds(0, NB - 1)]
    pltpu.make_async_copy(whole, whole, a2r.at[0]).wait()
    got = R[...].reshape(1024, 128)

    def decode(which):
        return lax.dot_general(got, D[which], (((0,), (0,)), ((), ())), preferred_element_type=F32)

    FS[...] = decode(1).astype(BF)
    far_out = pltpu.make_async_remote_copy(
        src_ref=FS, dst_ref=FR, send_sem=pss.at[1], recv_sem=psr.at[1],
        device_id=partner, device_id_type=MESH)
    far_out.start()
    far = decode(0)
    near_out.wait()
    for q in range(4):
        for ro in range(2):
            out_ref[q, ro] = (far[32 * q:32 * q + 32, 128 * ro:128 * ro + 128]
                              + NEAR[q, ro, :, pl.ds(mine, 128)] + NR[q, ro])
    sent = SEND.at[pl.ds(0, NB - 1)]
    pltpu.make_async_copy(sent, sent, a2s.at[0]).wait()
    for cp in started:
        cp.wait_send()
    far_out.wait()
    for q in range(4):
        for ro in range(2):
            out_ref[q, ro] += FR[32 * q:32 * q + 32, 128 * ro:128 * ro + 128].astype(F32)


def on_device(sources, encode, kernel, decode, near_blocks, near_list, near_mask, box_cell):
    smem = pl.BlockSpec(memory_space=pltpu.SMEM)
    hbm = pl.BlockSpec(memory_space=pl.ANY)
    vm = pl.BlockSpec(memory_space=pltpu.VMEM)
    n_sem = 2 * HALF
    return pl.pallas_call(
        body,
        out_shape=jax.ShapeDtypeStruct((PER, 2, RHS, 128), F32),
        in_specs=[smem, smem, vm, hbm, hbm, hbm, hbm, hbm],
        out_specs=vm,
        scratch_shapes=[
            pltpu.VMEM((258, 64, SZ), BF),
            pltpu.VMEM((1024, 128), F32),
            pltpu.VMEM((KD, 2, 2, 256, 256), BF),
            pltpu.VMEM((2, 1024, 256), BF),
            pltpu.VMEM((1024, 128), F32),
            pltpu.VMEM((NB, 16, 128), BF),
            pltpu.VMEM((NB, 16, 128), BF),
            pltpu.VMEM((PER, SLOTS, 512, SZ), BF),
            pltpu.VMEM((PER, 2, RHS, SZ), F32),
            pltpu.VMEM((PER, 2, RHS, 128), F32),
            pltpu.VMEM((PER, 2, RHS, 128), F32),
            pltpu.VMEM((128, 256), BF),
            pltpu.VMEM((128, 256), BF),
            pltpu.VMEM((256, 256), BF),
            pltpu.VMEM((256, 256), BF),
            pltpu.VMEM((256, 512), F32),
            pltpu.VMEM((2, 16, SZ), BF),
            pltpu.VMEM((16, SZ), BF),
            pltpu.VMEM((KD, 2, 16, 128), F32),
            pltpu.VMEM((2, 512, SZ), BF),
            pltpu.SemaphoreType.DMA((n_sem,)),
            pltpu.SemaphoreType.DMA((n_sem,)),
            pltpu.SemaphoreType.DMA((2,)),
            pltpu.SemaphoreType.DMA((PER,)),
            pltpu.SemaphoreType.DMA((3,)),
            pltpu.SemaphoreType.DMA((1,)),
            pltpu.SemaphoreType.DMA((1,)),
            pltpu.SemaphoreType.DMA((2,)),
            pltpu.SemaphoreType.DMA((2,)),
            pltpu.SemaphoreType.REGULAR,
        ],
        compiler_params=pltpu.CompilerParams(
            collective_id=0, has_side_effects=True, vmem_limit_bytes=56 * 2**20),
        name="fmm",
    )(near_list, near_mask, box_cell.reshape(1, 256), sources.reshape(PER, 64, SZ), encode, kernel,
      decode, near_blocks.reshape(PER, SLOTS, 512, SZ))


def solution(mesh):
    in_specs = (
        P("box", None, None, None),
        P(None, "dir", None),
        P(("dir", "box"), None, None, None),
        P(None, "dir", None),
        P("box", "dir", None, None, None),
        P("box", "dir"),
        P("box", "dir"),
        P(),
    )
    return jax.shard_map(
        on_device, mesh=mesh, in_specs=in_specs, out_specs=P("box", None, None, "dir"),
        check_vma=False)
```

```python
import jax
import jax.numpy as jnp
from jax import lax
from jax.experimental import pallas as pl
from jax.experimental.pallas import tpu as pltpu
from jax.sharding import PartitionSpec as P

MESH = pl.DeviceIdType.MESH
BF = jnp.bfloat16
F32 = jnp.float32

NB = 64
PER = 4
KD = 8
RHS = 32
SLOTS = 14
SZ = 256

ZX = 0
P1 = 1
F1 = 5
P2 = 7
F2 = 23
SIB = 31
PX = 47
HALF = 59
OFFS = (0, -1, 1, 2)


def box_of_input(i):
    w, j = i // 128, i % 128
    h, c, p2, p1, z = j // 64, j // 32 % 2, j // 8 % 4, j // 2 % 4, j % 2
    y = jnp.where(h == 0, p2, p1)
    x = jnp.where(h == 0, p1, p2)
    return (((y * 2 + z) * 4 + x) * 2 + c) * 4 + 2 * h + w


def slot_of_box(v):
    w, h, c = lax.rem(v, 2), lax.rem(v // 2, 2), lax.rem(v // 4, 2)
    x, z, y = lax.rem(v // 8, 4), lax.rem(v // 32, 2), v // 64
    first = 8 * y + 2 * x
    second = 8 * x + 2 * y
    return 2 * (h * 64 + c * 32 + jnp.where(h == 1, second, first) + z) + w


def dot_nt(a, b):
    return lax.dot_general(a, b, (((1,), (1,)), ((), ())), preferred_element_type=F32)


def body(list_ref, mask_ref, cell_ref, src_ref, enc_hbm, ker_hbm, dec_hbm, nb_hbm, out_ref,
         S, W, TT, D, V, SEND, R, NBV, NEAR, FS, FR, QI, QO, BASE, ENC2, E16, KER, DEC,
         ssem, rsem, lsem, nsem, isem, a2s, a2r, pss, psr, ready):
    bi = lax.axis_index("box")
    zl = lax.axis_index("dir")
    c = lax.rem(bi, 2)
    x = lax.rem(bi // 2, 4)
    zh = lax.rem(bi // 8, 2)
    y = bi // 16

    def dev(y_, zh_, x_, c_):
        return ((y_ * 2 + zh_) * 4 + x_) * 2 + c_

    def wrap(v):
        return lax.rem(v + 8, 4)

    zpart = (dev(y, 1 - zh, x, c), 1 - zl)
    sib = (dev(y, zh, x, 1 - c), zl)
    partner = (bi, 1 - zl)

    right, left = (dev(y, zh, wrap(x + 1), c), zl), (dev(y, zh, wrap(x - 1), c), zl)
    up, down = (dev(wrap(y + 1), zh, x, c), zl), (dev(wrap(y - 1), zh, x, c), zl)
    bar = pltpu.get_barrier_semaphore()
    for other in (right, left, up, down, zpart, sib, partner):
        pl.semaphore_signal(bar, inc=1, device_id=other, device_id_type=MESH)

    in_copies = [
        pltpu.make_async_copy(enc_hbm.at[:, pl.ds(pl.multiple_of(16 * (bi // 2), 16), 16), :], ENC2, isem.at[0]),
        pltpu.make_async_copy(ker_hbm, KER, isem.at[1]),
        pltpu.make_async_copy(dec_hbm, DEC, isem.at[2])]
    for cp in in_copies:
        cp.start()
    nb_copies = [pltpu.make_async_copy(nb_hbm.at[q], NBV.at[q], nsem.at[q]) for q in range(PER)]
    for cp in nb_copies:
        cp.start()
    pl.semaphore_wait(bar, 7)

    def pos(h):
        return (x, y) if h == 0 else (y, x)

    def ring(h, level, side):
        step = 1 if side == 0 else -1
        along_x = (h == 0) == (level == 1)
        if along_x:
            return (dev(y, zh, wrap(x + step), c), zl)
        return (dev(wrap(y + step), zh, x, c), zl)

    def sub(h, c_, p2, p1, z):
        return h * 64 + c_ * 32 + p2 * 8 + p1 * 2 + z

    def zof(which):
        return zh if which == 0 else 1 - zh

    def at(j, n=1):
        return S.at[pl.ds(2 * j, 2 * n)]

    started = []

    def copy(h, num, src, dst, device):
        cp = pltpu.make_async_remote_copy(
            src_ref=src, dst_ref=dst,
            send_sem=ssem.at[h * HALF + num], recv_sem=rsem.at[h * HALF + num],
            device_id=device, device_id_type=MESH)
        started.append(cp)
        held[h].append(cp)

    held = ([], [])

    def flush():
        a, b = held
        for n in range(max(len(a), len(b))):
            for side in (a, b):
                if n < len(side):
                    side[n].start()
        a.clear()
        b.clear()

    def send(h, num, j, device, n=1, src=None):
        copy(h, num, at(j, n) if src is None else src, at(j, n), device)

    def send_box(h, num, j, device, src=None):
        one = S.at[pl.ds(2 * j + zl, 1)]
        copy(h, num, one if src is None else src, one, device)

    def recv(h, num, boxes=2):
        k = h * HALF + num
        pltpu.make_async_copy(S.at[pl.ds(0, boxes)], S.at[pl.ds(0, boxes)], rsem.at[k]).wait()

    def spot(h, drow, piece, which):
        a, b = pos(h)
        return sub(h, c, wrap(b + OFFS[drow]), wrap(a + OFFS[piece]), zof(which))

    def p2_send(h, piece, which, src=None):
        j = spot(h, 0, piece, which)
        for side in (0, 1):
            num = P2 + 4 * piece + 2 * which + side
            if piece < 2:
                send_box(h, num, j, ring(h, 2, side), src)
            else:
                send(h, num, j, ring(h, 2, side), src=src)

    def p2_recv(h, piece, which):
        for side in (0, 1):
            recv(h, P2 + 4 * piece + 2 * which + side, 1 if piece < 2 else 2)

    def f2_send(h, piece, which):
        j = spot(h, 1 if which == 0 else 2, piece, which)
        num = F2 + 2 * piece + which
        if piece < 2:
            send_box(h, num, j, ring(h, 2, which))
        else:
            send(h, num, j, ring(h, 2, which))

    def f2_recv(h, piece):
        for side in (0, 1):
            recv(h, F2 + 2 * piece + side, 1 if piece < 2 else 2)

    def px_send(h, piece, drow, which):
        send_box(h, PX + 6 * piece + 2 * (drow - 1) + which, spot(h, drow, piece, which),
                 partner if piece == 0 else zpart)

    def px_recv(h, piece, drow):
        for which in (0, 1):
            recv(h, PX + 6 * piece + 2 * (drow - 1) + which, 1)

    def encode(j0):
        rows = S[pl.ds(2 * j0, 4)].reshape(256, SZ)
        o = dot_nt(E16[...], rows)
        top, low = o[0:8], o[8:16]
        lane = lax.broadcasted_iota(jnp.int32, (8, 128), 1) % 64
        for half in range(2):
            t = top[:, 128 * half:128 * half + 128]
            u = low[:, 128 * half:128 * half + 128]
            turned = jnp.where(lane < 32, -pltpu.roll(u, 96, 1), pltpu.roll(u, 32, 1))
            W[pl.ds(pl.multiple_of(8 * j0 + 8 * half, 8), 8), :] = t + turned

    def pair(h, c_, drow, piece):
        a, b = pos(h)
        return sub(h, c_, wrap(b + OFFS[drow]), wrap(a + OFFS[piece]), 0)

    earlier = []

    def finish(pairs):
        flush()
        for h, drow, piece in pairs:
            send(h, SIB + 4 * drow + piece, pair(h, c, drow, piece), sib, n=2)
        flush()
        for h, drow, piece in pairs:
            encode(pair(h, c, drow, piece))
        for h, drow, piece in earlier:
            recv(h, SIB + 4 * drow + piece, 4)
        for h, drow, piece in earlier:
            encode(pair(h, 1 - c, drow, piece))
        earlier[:] = pairs

    local = []
    for h in (0, 1):
        own = spot(h, 0, 0, 0)
        src = src_ref.at[pl.ds(2 * h, 2)]
        for side in (0, 1):
            send(h, P1 + side, own, ring(h, 1, side), src=src)
        send(h, ZX, own, zpart, src=src)
        cp = pltpu.make_async_copy(src, at(own), lsem.at[h])
        cp.start()
        local.append(cp)
    for h in (0, 1):
        p2_send(h, 0, 0, src=src_ref.at[pl.ds(2 * h + zl, 1)])
    flush()

    S[pl.ds(256, 2)] = jnp.zeros((2, 64, SZ), BF)
    cell = cell_ref[...]
    cx, cy, cz = cell // 32, cell // 4 % 8, cell % 4
    cell_in = cx * 32 + cz * 8 + cy
    row = lax.broadcasted_iota(jnp.int32, (256, 256), 0)
    col = lax.broadcasted_iota(jnp.int32, (256, 256), 1)
    row1 = lax.broadcasted_iota(jnp.int32, (256, 1), 0)

    def hot(cond):
        return jnp.where(cond, 1.0, 0.0).astype(BF)

    QI[...] = dot_nt(hot(box_of_input(row1) == col), hot(row == cell_in)).astype(BF)
    QO[...] = dot_nt(hot(4 * (row1 % 64) + row1 // 64 == col), hot(row == cell)).astype(BF)

    in_copies[0].wait()
    two_rows = ENC2[...].astype(F32)
    E16[...] = jnp.where(lax.rem(bi, 2) == 1, two_rows[:, 8:16], two_rows[:, 0:8]).reshape(16, SZ).astype(BF)

    in_copies[1].wait()
    d_i = lax.broadcasted_iota(jnp.int32, (256, 128), 0) % 16
    l_i = lax.broadcasted_iota(jnp.int32, (256, 128), 1)
    ly, lz = l_i // 8, l_i % 8
    close = (((d_i <= 1) | (d_i == 15)) & ((ly <= 1) | (ly == 15)) & ((lz <= 1) | (lz == 7)))
    kept = jnp.where(close, 0.0, KER[...].reshape(256, 128))
    k_hi = kept.astype(BF)
    k_lo = (kept - k_hi.astype(F32)).astype(BF)
    lane512 = lax.broadcasted_iota(jnp.int32, (128, 512), 1)
    take = (lane512 % 64) // 4 * 8 + (lane512 % 4 - lane512 // 128 + 8) % 8
    spread = hot(lax.broadcasted_iota(jnp.int32, (128, 512), 0) == take)
    BASE[...] = (jnp.dot(k_hi, spread, preferred_element_type=F32)
                 + jnp.dot(k_lo, spread, preferred_element_type=F32))

    def build_d(mine):
        col = pl.multiple_of(128 * (zl if mine else 1 - zl), 128)
        dr = DEC[0, :, pl.ds(col, 128)].astype(F32).reshape(64, 1, 8, 128)
        di = DEC[1, :, pl.ds(col, 128)].astype(F32).reshape(64, 1, 8, 128)
        left = jnp.concatenate([dr, -di], axis=1).reshape(1024, 128)
        right = jnp.concatenate([di, dr], axis=1).reshape(1024, 128)
        D[0 if mine else 1] = jnp.concatenate([left, right], axis=1).astype(BF)

    lane = lax.broadcasted_iota(jnp.int32, (8, 128), 1)

    def build_t(k):
        for ri in range(2):
            rows = BASE[pl.ds(pl.multiple_of(32 * k + 16 * ri, 16), 16), :]
            one, two = {}, {}
            for dx in range(-7, 8):
                line = rows[dx % 16:dx % 16 + 1, :]
                one[dx] = [pltpu.roll(jnp.broadcast_to(line[:, 128 * s:128 * s + 128], (8, 128)),
                                      0, 1, stride=4, stride_axis=0) for s in range(4)]
            for d in range(-7, 7):
                two[d] = [jnp.where(lane % 64 < 32, one[d][s], pltpu.roll(one[d + 1][s], 32, 1))
                          for s in range(4)]
            four = {d: [jnp.where(lane < 64, two[d][s], two[d + 2][s]) for s in range(4)]
                    for d in range(-7, 5)}
            wide = jnp.concatenate([
                jnp.concatenate([four[-sx][s], four[4 - sx][s]], axis=1)
                for sx in range(8) for s in range(4)], axis=0)
            hi = wide.astype(BF)
            lo = (wide - hi.astype(F32)).astype(BF)
            for part, val in enumerate((hi, lo)):
                first = dot_nt(QO[...], val).astype(BF)
                TT[k, part, ri] = dot_nt(first, QI[...]).astype(BF)

    def step_t(k):
        flush()
        lax.fori_loop(k, k + 1, lambda n, _: (build_t(n), 0)[1], 0)

    def step_t(k):
        flush()
        lax.fori_loop(k, k + 1, lambda n, _: (build_t(n), 0)[1], 0)

    for cp in local:
        cp.wait()
    both = (0, 1)

    def p2_relay(h, piece, which):
        p2_recv(h, piece, which)
        if piece < 2:
            px_send(h, piece, 1, which)
            px_send(h, piece, 2, which)
        f2_send(h, piece, which)

    def f2_relay(h, piece):
        f2_recv(h, piece)
        px_send(h, piece, 3, 0)
        px_send(h, piece, 3, 1)

    def relay(*steps):
        for piece, which in steps:
            for h in both:
                p2_relay(h, piece, which)
            flush()

    for h in both:
        for side in both:
            recv(h, P1 + side)
        send(h, F1, spot(h, 0, 1, 0), ring(h, 1, 0))
    flush()
    for h in both:
        recv(h, ZX)
        for side in both:
            send(h, P1 + 2 + side, spot(h, 0, 0, 1), ring(h, 1, side))
    flush()
    for h in both:
        p2_send(h, 1, 0)
        p2_send(h, 0, 1)
        p2_send(h, 2, 0)
    flush()
    relay((0, 0))
    finish([(h, 0, 0) for h in both])
    step_t(0)
    step_t(1)
    for h in both:
        for side in both:
            recv(h, P1 + 2 + side)
        send(h, F1 + 1, spot(h, 0, 2, 1), ring(h, 1, 1))
    flush()
    for h in both:
        recv(h, F1)
        p2_send(h, 3, 0)
    flush()
    for h in both:
        p2_send(h, 1, 1)
        p2_send(h, 2, 1)
    finish([(h, 0, piece) for piece in (1, 2) for h in both])
    relay((0, 1), (1, 0))
    step_t(2)
    step_t(3)
    for h in both:
        recv(h, F1 + 1)
        p2_send(h, 3, 1)
    finish([(h, 0, 3) for h in both])
    step_t(4)
    step_t(5)
    in_copies[2].wait()
    build_d(False)
    build_d(True)
    for h in both:
        f2_relay(h, 0)
    flush()
    relay((2, 0), (1, 1))
    step_t(6)
    relay((3, 0), (2, 1))
    finish([(h, drow, 2) for drow in (1, 2) for h in both])
    step_t(7)
    for h in both:
        f2_relay(h, 1)
    flush()
    relay((3, 1))
    finish([(h, drow, 3) for drow in (1, 2) for h in both])
    for h in both:
        for drow in (1, 2):
            px_recv(h, 0, drow)
    finish([(h, drow, 0) for drow in (1, 2) for h in both])
    flush()
    for h in both:
        for drow in (1, 2):
            px_recv(h, 1, drow)
    finish([(h, drow, 1) for drow in (1, 2) for h in both])
    flush()
    flush()
    for h in both:
        px_recv(h, 0, 3)
        f2_recv(h, 2)
    finish([(h, 3, piece) for piece in (0, 2) for h in both])
    for h in both:
        px_recv(h, 1, 3)
    finish([(h, 3, 1) for h in both])
    for h in both:
        f2_recv(h, 3)
    finish([(h, 3, 3) for h in both])
    finish([])

    pl.semaphore_signal(ready, inc=1, device_id=partner, device_id_type=MESH)
    lane64 = lax.broadcasted_iota(jnp.int32, (256, 64), 1)
    quarter = lax.broadcasted_iota(jnp.int32, (64, 128), 1) // 32

    def translate(k, _):
        v = W[pl.ds(k, 128, stride=8), :]
        e = jnp.concatenate([v[:, 0:64], v[:, 64:128]], axis=0)
        hi = e.astype(BF)
        lo = (e - hi.astype(F32)).astype(BF)
        t_hi = TT[k, 0].reshape(512, 256)
        t_lo = TT[k, 1].reshape(512, 256)
        nn = (((1,), (0,)), ((), ()))
        wide = lax.dot_general(t_hi, jnp.concatenate([hi, lo], axis=1), nn, preferred_element_type=F32)
        f = wide[:, 0:64] + wide[:, 64:128]
        f = f + lax.dot_general(t_lo, hi, nn, preferred_element_type=F32)
        fr, fi = f[0:256], f[256:512]
        swapped = jnp.concatenate([fi[:, 32:64], fi[:, 0:32]], axis=1)
        far = fr + jnp.where(lane64 < 32, -swapped, swapped)
        far = jnp.concatenate([far, far], axis=1)
        far_sw = pltpu.roll(far, 32, 1)
        for ri in range(2):
            val = None
            for q in range(4):
                use = far if (q - ri) % 2 == 0 else far_sw
                block = use[64 * q:64 * q + 64]
                val = block if val is None else jnp.where(quarter == q, block, val)
            V[pl.ds(8 * ri + k, 64, stride=16), :] = val
        return 0

    lax.fori_loop(0, KD, translate, 0, unroll=4)
    SEND[...] = V[...].astype(BF).reshape(64, 16, 128)
    R[pl.ds(bi, 1)] = SEND[pl.ds(bi, 1)]

    def scatter(t, _):
        dst = lax.rem(bi + t, NB)
        pltpu.make_async_remote_copy(
            src_ref=SEND.at[dst], dst_ref=R.at[bi], send_sem=a2s.at[0], recv_sem=a2r.at[0],
            device_id=(dst, zl), device_id_type=MESH).start()
        return 0

    pl.semaphore_wait(ready, 1)
    lax.fori_loop(1, NB, scatter, 0)

    def near_box(q, _):
        blocks = NBV[q]
        xs = jnp.concatenate(
            [S[jnp.where(mask_ref[q, s] == 1, slot_of_box(list_ref[q, s]), 256)]
             for s in range(SLOTS)], axis=1)
        bs = jnp.concatenate([blocks[s] for s in range(SLOTS)], axis=1)
        n = dot_nt(xs, bs)
        NEAR[q, 0] = n[0:32, 0:256] - n[32:64, 256:512]
        NEAR[q, 1] = n[32:64, 0:256] + n[0:32, 256:512]
        return 0

    for cp in nb_copies:
        cp.wait()
    lax.fori_loop(0, PER, near_box, 0)

    mine = pl.multiple_of(128 * zl, 128)
    theirs = pl.multiple_of(128 * (1 - zl), 128)

    for cp in started:
        cp.wait_send()
    whole = R.at[pl.ds(0, NB - 1)]
    sent = SEND.at[pl.ds(0, NB - 1)]
    pltpu.make_async_copy(sent, sent, a2s.at[0]).wait()
    pltpu.make_async_copy(whole, whole, a2r.at[0]).wait()
    got = R[...].reshape(1024, 128)

    def decode(which):
        return lax.dot_general(got, D[which], (((0,), (0,)), ((), ())), preferred_element_type=F32)

    far = decode(1)
    for q in range(4):
        for ro in range(2):
            FS[32 * q:32 * q + 32, 128 * ro:128 * ro + 128] = (
                far[32 * q:32 * q + 32, 128 * ro:128 * ro + 128]
                + NEAR[q, ro, :, pl.ds(theirs, 128)]).astype(BF)
    far_out = pltpu.make_async_remote_copy(
        src_ref=FS, dst_ref=FR, send_sem=pss.at[0], recv_sem=psr.at[0],
        device_id=partner, device_id_type=MESH)
    far_out.start()
    far = decode(0)
    for q in range(4):
        for ro in range(2):
            out_ref[q, ro] = (far[32 * q:32 * q + 32, 128 * ro:128 * ro + 128]
                              + NEAR[q, ro, :, pl.ds(mine, 128)])
    far_out.wait()
    for q in range(4):
        for ro in range(2):
            out_ref[q, ro] += FR[32 * q:32 * q + 32, 128 * ro:128 * ro + 128].astype(F32)


def on_device(sources, encode, kernel, decode, near_blocks, near_list, near_mask, box_cell):
    smem = pl.BlockSpec(memory_space=pltpu.SMEM)
    hbm = pl.BlockSpec(memory_space=pl.ANY)
    vm = pl.BlockSpec(memory_space=pltpu.VMEM)
    n_sem = 2 * HALF
    return pl.pallas_call(
        body,
        out_shape=jax.ShapeDtypeStruct((PER, 2, RHS, 128), F32),
        in_specs=[smem, smem, vm, hbm, hbm, hbm, hbm, hbm],
        out_specs=vm,
        scratch_shapes=[
            pltpu.VMEM((258, 64, SZ), BF),
            pltpu.VMEM((1024, 128), F32),
            pltpu.VMEM((KD, 2, 2, 256, 256), BF),
            pltpu.VMEM((2, 1024, 256), BF),
            pltpu.VMEM((1024, 128), F32),
            pltpu.VMEM((NB, 16, 128), BF),
            pltpu.VMEM((NB, 16, 128), BF),
            pltpu.VMEM((PER, SLOTS, 512, SZ), BF),
            pltpu.VMEM((PER, 2, RHS, SZ), F32),
            pltpu.VMEM((128, 256), BF),
            pltpu.VMEM((128, 256), BF),
            pltpu.VMEM((256, 256), BF),
            pltpu.VMEM((256, 256), BF),
            pltpu.VMEM((256, 512), F32),
            pltpu.VMEM((2, 16, SZ), BF),
            pltpu.VMEM((16, SZ), BF),
            pltpu.VMEM((KD, 2, 16, 128), F32),
            pltpu.VMEM((2, 512, SZ), BF),
            pltpu.SemaphoreType.DMA((n_sem,)),
            pltpu.SemaphoreType.DMA((n_sem,)),
            pltpu.SemaphoreType.DMA((2,)),
            pltpu.SemaphoreType.DMA((PER,)),
            pltpu.SemaphoreType.DMA((3,)),
            pltpu.SemaphoreType.DMA((1,)),
            pltpu.SemaphoreType.DMA((1,)),
            pltpu.SemaphoreType.DMA((1,)),
            pltpu.SemaphoreType.DMA((1,)),
            pltpu.SemaphoreType.REGULAR,
        ],
        compiler_params=pltpu.CompilerParams(
            collective_id=0, has_side_effects=True, vmem_limit_bytes=56 * 2**20),
        name="fmm",
    )(near_list, near_mask, box_cell.reshape(1, 256), sources.reshape(PER, 64, SZ), encode, kernel,
      decode, near_blocks.reshape(PER, SLOTS, 512, SZ))


def solution(mesh):
    in_specs = (
        P("box", None, None, None),
        P(None, "dir", None),
        P(("dir", "box"), None, None, None),
        P(None, "dir", None),
        P("box", "dir", None, None, None),
        P("box", "dir"),
        P("box", "dir"),
        P(),
    )
    return jax.shard_map(
        on_device, mesh=mesh, in_specs=in_specs, out_specs=P("box", None, None, "dir"),
        check_vma=False)
```
